32 devices in a mesh: dp: 8 (over z, y), tensor: 4 (over x, core).
Axes of the slice: x: 2, y: 2, z: 4, core: 2. Of those that a mesh axis runs over, the one named last changes fastest.
Arguments:
- tokens: bfloat16 [2048, 4096], P('dp', 'tensor'), may hold values from -24 to 24
- segments: int32 [16, 128], P('dp'), may hold values from 0 to 3, never falling along the last dimension, each value on 1 to 96 neighbouring positions
- w_query: bfloat16 [4096, 4096], P('dp', 'tensor'), may hold values from -1 to 1
- key_weight: bfloat16 [4096, 1024], P('dp', 'tensor'), may hold values from -1 to 1
- value_weight: bfloat16 [4096, 1024], P('dp', 'tensor'), may hold values from -0.09375 to 0.09375
- w_out: bfloat16 [4096, 4096], P('dp', 'tensor'), may hold values from -0.375 to 0.375
- w_gate: bfloat16 [4096, 12288], P('dp', 'tensor'), may hold values from -0.09375 to 0.09375
- w_up: bfloat16 [4096, 12288], P('dp', 'tensor'), may hold values from -0.09375 to 0.09375
- w_down: bfloat16 [4096, 12288], P('dp', 'tensor'), may hold values from -0.0546875 to 0.0546875
- attn_gain: float32 [4096], P(('dp', 'tensor')), may hold values from 0.25 to 1.75
- ffn_gain: float32 [4096], P(('dp', 'tensor')), may hold values from 0.25 to 1.75
- query_norm_gain: float32 [128], replicated, may hold values from 0.6 to 5
- key_gain: float32 [128], replicated, may hold values from 0.6 to 5
- cotangent: bfloat16 [2048, 4096], P('dp', 'tensor'), may hold values from -6 to 6
Outputs:
- block_out: bfloat16 [2048, 4096], P('dp', 'tensor')
- tokens_grad: float32 [2048, 4096], P('dp', 'tensor')
- w_query_grad: float32 [4096, 4096], P('dp', 'tensor')
- w_key_grad: float32 [4096, 1024], P('dp', 'tensor')
- w_value_grad: float32 [4096, 1024], P('dp', 'tensor')
- w_out_grad: float32 [4096, 4096], P('dp', 'tensor')
- w_gate_grad: float32 [4096, 12288], P('dp', 'tensor')
- w_up_grad: float32 [4096, 12288], P('dp', 'tensor')
- w_down_grad: float32 [4096, 12288], P('dp', 'tensor')
- attn_gain_grad: float32 [4096], P(('dp', 'tensor'))
- ffn_gain_grad: float32 [4096], P(('dp', 'tensor'))
- query_gain_grad: float32 [128], replicated
- key_gain_grad: float32 [128], replicated
The draws below stay inside these ranges and needn't reach their ends.
Inputs may be any that keep to these rules, and one draw needn't show every extreme that they name: `segments`: in each row (one micro-batch) the sequence numbers never fall, every number of 0 to 3 occurs, each sequence holds 1 to 96 rows, and one holds exactly that many.
All inputs are finite; a program needn't handle non-finite values.
Results may differ from the reference program's by a relative error of at most 0.017.
The reference program's roundings to bfloat16 on the way count: a program that leaves them out, or rounds other values in their place, can miss the bound.
Values may be sent and summed in bfloat16 or wider, within the bound.
No kernel may reach another device: no remote copies, remote signals or barrier semaphores. Data moves between devices by JAX's collectives and lax.ppermute only.
A program may use at most 384 MiB of HBM per device.

```python
import math
import jax
import jax.numpy as jnp
import numpy as np
from jax import lax

MODEL_DIM = 4096
QUERY_HEAD_COUNT = 32
KEY_VALUE_HEADS = 8
HEAD_DIM = 128
FF = 12288
MBTOK = 128
MB = 2
NSEG = 4
TOKENS = 2048
N_DP = 8


def query_width(key):
    value_rows = jax.random.normal(jax.random.fold_in(key, 21), (MODEL_DIM, QUERY_HEAD_COUNT * HEAD_DIM), jnp.float32)
    return jnp.clip(value_rows, -6.0, 6.0) * MODEL_DIM ** (-0.5)


def draw_w_query(key, part):
    return query_width(key).astype(jnp.bfloat16)


def draw_key_weight(key, part):
    value_rows = jax.random.normal(jax.random.fold_in(key, 22), (MODEL_DIM, KEY_VALUE_HEADS * HEAD_DIM), jnp.float32)
    independent = jnp.clip(value_rows, -6.0, 6.0) * MODEL_DIM ** (-0.5)
    return independent.astype(jnp.bfloat16)


def draw_query_norm_gain(key, part):
    return jax.random.uniform(jax.random.fold_in(key, 31), (HEAD_DIM,), jnp.float32, 0.6, 1.4)


def draw_key_gain(key, part):
    return jax.random.uniform(jax.random.fold_in(key, 32), (HEAD_DIM,), jnp.float32, 0.6, 1.4)


def draw_tokens(key, part):
    value_rows = jax.random.normal(jax.random.fold_in(key, 41), (TOKENS, MODEL_DIM), jnp.float32)
    return jnp.clip(value_rows, -6.0, 6.0).astype(jnp.bfloat16)


def with_spikes(values, stream_key, source, target, blocks, factor):
    def block_of(dim):
        return (jnp.arange(values.shape[dim]) // (values.shape[dim] // blocks)).reshape((-1,) + (1,) * (values.ndim - 1 - dim))

    near = jax.random.permutation(stream_key, blocks)[block_of(target)]
    other_side = (block_of(target) + blocks // 2) % blocks
    return jnp.where((block_of(source) == near) | (block_of(source) == other_side), factor * values, values)


def block_levels(key, shape, shards, least, high):
    gain = 1.0
    for axis_at, shards_of in shards:
        draws = jax.random.uniform(jax.random.fold_in(jax.random.fold_in(key, 6), axis_at), (shards_of,), jnp.float32, least / len(shards), high / len(shards))
        gain = gain * jnp.repeat(jnp.exp(draws), shape[axis_at] // shards_of).reshape((-1,) + (1,) * (len(shape) - 1 - axis_at))
    return gain


def split_up(count, total, limit, skew):
    weights = [(1 << 20) // math.isqrt(grade ** skew) + 1 for grade in range(2, count + 1)]
    rest, holding = total - limit - (count - 1), [1] * (count - 1)
    while rest > 0:
        free = [i for i in range(count - 1) if holding[i] < limit]
        mass, remaining = sum([weights[i] for i in free]), rest
        for i in free:
            addition = min(limit - holding[i], max(1, remaining * weights[i] // mass), rest)
            holding[i] = holding[i] + addition
            rest = rest - addition
    return np.array([limit] + holding)


def ragged_sizes(own_key, number_of, total, bound, lean):
    if number_of == 2:
        one = jax.random.randint(own_key, (), max(1, total - bound), min(bound, total - 1) + 1)
        return jnp.stack([one, total - one])
    lengths = jnp.asarray(split_up(number_of, total, bound, lean), jnp.int32)
    pairs = (number_of - 1) // 2
    source_of, receiver = lengths[1:1 + 2 * pairs:2], lengths[2:2 + 2 * pairs:2]
    slack = jnp.minimum(source_of - 1, bound - receiver)
    shifted = jax.random.randint(jax.random.fold_in(own_key, 1), (pairs,), 0, 1 << 20) % (slack + 1)
    lengths = lengths.at[1:1 + 2 * pairs:2].set(source_of - shifted).at[2:2 + 2 * pairs:2].set(receiver + shifted)
    return lengths[jax.random.permutation(jax.random.fold_in(own_key, 2), number_of)]


def gaussian(stream_key, shape, spread, bound, pieces=(), kind=jnp.bfloat16):
    result = spread * jax.random.normal(stream_key, shape, jnp.float32)
    if pieces:
        result = result * block_levels(stream_key, shape, pieces, -0.22, 0.18)
    return jnp.clip(result, -bound, bound).astype(kind)


def heavy_noise(rng, extent, deviation, limit, cuts, heavy, held_as=jnp.bfloat16):
    entries = deviation * jax.random.normal(rng, extent, jnp.float32)
    if cuts:
        entries = entries * block_levels(rng, extent, cuts, -0.22, 0.18)
    return jnp.clip(with_spikes(entries, jax.random.fold_in(rng, 3), *heavy), -limit, limit).astype(held_as)


def setup_inputs(seed: int = 0) -> dict:
    arg_keys = jax.random.split(jax.random.key(seed), 15)
    tokens = draw_tokens(jax.random.fold_in(arg_keys[14], 71), 0)
    segments = jax.vmap(lambda own: jnp.searchsorted(jnp.cumsum(ragged_sizes(own, NSEG, MBTOK, 3 * MBTOK // 4, 2)), jnp.arange(MBTOK), side="right"))(jax.random.split(arg_keys[1], (N_DP * MB))).reshape((N_DP * MB, MBTOK)).astype(jnp.int32)
    w_query = draw_w_query(jax.random.fold_in(arg_keys[14], 71), 0)
    key_weight = draw_key_weight(jax.random.fold_in(arg_keys[14], 71), 0)
    value_weight = gaussian(arg_keys[4], (MODEL_DIM, KEY_VALUE_HEADS * HEAD_DIM), MODEL_DIM ** -0.5, 0.09375, ((0, 8), (1, 4)))
    w_out = gaussian(arg_keys[5], (MODEL_DIM, QUERY_HEAD_COUNT * HEAD_DIM), (QUERY_HEAD_COUNT * HEAD_DIM // 16) ** -0.5, 0.375, ((0, 8), (1, 4)))
    w_gate = gaussian(arg_keys[6], (MODEL_DIM, FF), MODEL_DIM ** -0.5, 0.09375, ((0, 8), (1, 4)))
    w_up = gaussian(arg_keys[7], (MODEL_DIM, FF), MODEL_DIM ** -0.5, 0.09375, ((0, 8), (1, 4)))
    w_down = gaussian(arg_keys[8], (MODEL_DIM, FF), FF ** -0.5, 0.0546875, ((0, 8), (1, 4)))
    attn_gain = jnp.clip(1.0 + 0.15 * jax.random.normal(arg_keys[9], (MODEL_DIM,), jnp.float32), 0.25, 1.75)
    ffn_gain = jnp.clip(1.0 + 0.15 * jax.random.normal(arg_keys[10], (MODEL_DIM,), jnp.float32), 0.25, 1.75)
    query_norm_gain = draw_query_norm_gain(jax.random.fold_in(arg_keys[14], 71), 0)
    key_gain = draw_key_gain(jax.random.fold_in(arg_keys[14], 71), 0)
    cotangent = heavy_noise(arg_keys[13], (TOKENS, MODEL_DIM), 1.0, 6.0, ((0, 8), (1, 4)), (0, 1, 8, 2.0))
    return dict(tokens=tokens, segments=segments, w_query=w_query, key_weight=key_weight, value_weight=value_weight, w_out=w_out, w_gate=w_gate, w_up=w_up, w_down=w_down, attn_gain=attn_gain, ffn_gain=ffn_gain, query_norm_gain=query_norm_gain, key_gain=key_gain, cotangent=cotangent)


epsilon = 1e-06
rope_base = 1000000.0
masked_score = -1e+30

@jax.custom_vjp
def to_low_precision(v):
    return lax.optimization_barrier(v.astype(jnp.bfloat16)).astype(jnp.float32)

@jax.custom_vjp
def low_precision_back(v):
    return v

def low_keep(v):
    return (to_low_precision(v), None)

def low_pass(kept, grad):
    return (grad,)

def back_keep(v):
    return (v, None)

def back_low(kept, grad):
    return (to_low_precision(grad),)
to_low_precision.defvjp(low_keep, low_pass)
low_precision_back.defvjp(back_keep, back_low)

def rope_tables(segment):
    token_row_count = segment.shape[0]
    starts = lax.optimization_barrier(jnp.sum((segment[None, :] < segment[:, None]).astype(jnp.int32), axis=1))
    position = (jnp.arange(token_row_count, dtype=jnp.int32) - starts).astype(jnp.float32)
    half_size = HEAD_DIM // 2
    frequency = jnp.power(rope_base, -2.0 * jnp.arange(half_size, dtype=jnp.float32) / HEAD_DIM)
    angles = position[:, None] * frequency[None, :]
    angles = jnp.concatenate([angles, angles], axis=1)
    return (jnp.cos(angles)[:, None, :], jnp.sin(angles)[:, None, :])

def visible(segment):
    token_row_count = segment.shape[0]
    row_order = jnp.arange(token_row_count, dtype=jnp.int32)
    return (segment[:, None] == segment[None, :]) & (row_order[:, None] >= row_order[None, :])

def apply_rotary(value_rows, cosine_table, sine_table):
    half_size = value_rows.shape[-1] // 2
    turned = jnp.concatenate([-value_rows[..., half_size:], value_rows[..., :half_size]], axis=-1)
    return value_rows * cosine_table + turned * sine_table

def per_head_norm(value_rows, gain_vector):
    return value_rows * lax.rsqrt(lax.optimization_barrier(jnp.mean(value_rows * value_rows, axis=-1, keepdims=True)) + epsilon) * gain_vector

def decoder_layer(x_block, segment, params):
    w_query, key_weight, value_weight, w_out, w_gate, w_up, w_down, attn_gain, ffn_gain, query_norm_gain, key_gain = params
    highest_precision = lax.Precision.HIGHEST
    token_row_count = x_block.shape[0]
    head_groups = QUERY_HEAD_COUNT // KEY_VALUE_HEADS
    first_hidden = to_low_precision(x_block * lax.rsqrt(lax.optimization_barrier(jnp.mean(x_block * x_block, axis=-1, keepdims=True)) + epsilon) * attn_gain)
    query_before_norm = low_precision_back(jnp.dot(first_hidden, w_query, precision=highest_precision)).reshape(token_row_count, QUERY_HEAD_COUNT, HEAD_DIM)
    key_before_norm = low_precision_back(jnp.dot(first_hidden, key_weight, precision=highest_precision)).reshape(token_row_count, KEY_VALUE_HEADS, HEAD_DIM)
    value_reduced = to_low_precision(low_precision_back(jnp.dot(first_hidden, value_weight, precision=highest_precision))).reshape(token_row_count, KEY_VALUE_HEADS, HEAD_DIM)
    cosine_table, sine_table = rope_tables(segment)
    query_rotated = to_low_precision(apply_rotary(per_head_norm(query_before_norm, query_norm_gain), cosine_table, sine_table)).reshape(token_row_count, KEY_VALUE_HEADS, head_groups, HEAD_DIM)
    key_rot = to_low_precision(apply_rotary(per_head_norm(key_before_norm, key_gain), cosine_table, sine_table))
    scores = low_precision_back(jnp.einsum('qkgd,skd->kgqs', query_rotated, key_rot, precision=highest_precision) * HEAD_DIM ** (-0.5))
    scores = jnp.where(visible(segment)[None, None], scores, masked_score)
    top_score = lax.optimization_barrier(jnp.max(scores, axis=-1, keepdims=True))
    exp_scores = jnp.exp(scores - top_score)
    probability = exp_scores / lax.optimization_barrier(jnp.sum(exp_scores, axis=-1, keepdims=True))
    mixed_heads = jnp.einsum('kgqs,skd->qkgd', to_low_precision(probability), value_reduced, precision=highest_precision).reshape(token_row_count, QUERY_HEAD_COUNT * HEAD_DIM)
    mixed_heads = to_low_precision(low_precision_back(mixed_heads))
    attended = low_precision_back(jnp.dot(mixed_heads, w_out.T, precision=highest_precision))
    residual = x_block + attended
    hidden_two = to_low_precision(residual * lax.rsqrt(lax.optimization_barrier(jnp.mean(residual * residual, axis=-1, keepdims=True)) + epsilon) * ffn_gain)
    gate_pre = low_precision_back(jnp.dot(hidden_two, w_gate, precision=highest_precision))
    up_proj = low_precision_back(jnp.dot(hidden_two, w_up, precision=highest_precision))
    act_low = to_low_precision(jax.nn.silu(gate_pre) * up_proj)
    return residual + jnp.dot(act_low, w_down.T, precision=highest_precision)

def reference(tokens, segments, w_query, key_weight, value_weight, w_out, w_gate, w_up, w_down, attn_gain, ffn_gain, query_norm_gain, key_gain, cotangent):
    matrices = tuple((w.astype(jnp.float32) for w in (w_query, key_weight, value_weight, w_out, w_gate, w_up, w_down)))
    params = matrices + (attn_gain, ffn_gain, query_norm_gain, key_gain)
    blocks = tokens.astype(jnp.float32).reshape(N_DP * MB, MBTOK, MODEL_DIM)

    def forward(block_rows, layer_params):

        def scan_step(scan_carry, block_item):
            return (scan_carry, jax.checkpoint(decoder_layer)(block_item[0], block_item[1], layer_params))
        return lax.scan(scan_step, jnp.zeros((), jnp.float32), (block_rows, segments))[1]
    layer_out, pull_back = jax.vjp(forward, blocks, params)
    grad_rows, grad_params = pull_back(cotangent.astype(jnp.float32).reshape(N_DP * MB, MBTOK, MODEL_DIM))
    return (layer_out.reshape(TOKENS, MODEL_DIM).astype(jnp.bfloat16), grad_rows.reshape(TOKENS, MODEL_DIM), grad_params[0], grad_params[1], grad_params[2], grad_params[3], grad_params[4], grad_params[5], grad_params[6], grad_params[7], grad_params[8], grad_params[9], grad_params[10])
```

```python
import jax
import jax.numpy as jnp
from jax import lax
from jax.sharding import Mesh
from jax.sharding import PartitionSpec as P

epsilon = 1e-06
rope_base = 1000000.0
masked_score = -1e30
f32 = jnp.float32
bf16 = jnp.bfloat16


def shift(value, axis, step):
    size = lax.axis_size(axis)
    return lax.ppermute(value, axis, [(i, (i + step) % size) for i in range(size)])


def flip(value, axis, mask=1):
    return lax.ppermute(value, axis, [(i, i ^ mask) for i in range(lax.axis_size(axis))])


def transpose_blocks(value):
    size = lax.axis_size("a")
    inner = lax.axis_size("c")
    outer = lax.axis_size("x")
    pairs = []
    for a in range(size):
        for t in range(outer * inner):
            pairs.append((a * size + t, t * size + a))
    return lax.ppermute(value, ("a", "x", "c"), pairs)


def ring_sum(value):
    if lax.axis_size("a") != 4:
        return lax.psum(value, "a")
    value = value + flip(value, "a", 1)
    return value + flip(value, "a", 3)


def ring_scatter(partial):
    rows = partial.shape[0] // 4
    half = rows // 2
    one = partial[rows : 2 * rows]
    two = partial[2 * rows : 3 * rows]
    three = partial[3 * rows :]
    up_first = shift(two[:half], "a", 1)
    down_first = shift(two[half:], "a", -1)
    one = jnp.concatenate([one[:half] + up_first, one[half:]], axis=0)
    three = jnp.concatenate([three[:half], three[half:] + down_first], axis=0)
    return partial[:rows] + shift(one, "a", 1) + shift(three, "a", -1)


def ring_gather(own):
    half = own.shape[0] // 2
    from_before = shift(own, "a", 1)
    from_after = shift(own, "a", -1)
    top = shift(from_before[:half], "a", 1)
    bottom = shift(from_after[half:], "a", -1)
    return jnp.concatenate([own, from_after, top, bottom, from_before], axis=0)


def tensor_scatter(partial):
    size = lax.axis_size("a")
    a = lax.axis_index("a")
    x = lax.axis_index("x")
    c = lax.axis_index("c")
    rows = partial.shape[0] // size

    def block(t):
        return lax.dynamic_slice_in_dim(partial, ((t - a) % size) * rows, rows)

    send = jnp.stack([block(2 * (1 - x) + 1 - c), block(2 * x + 1 - c)])
    got = flip(send, "c")
    far = block(2 * (1 - x) + c) + got[0]
    near = block(2 * x + c) + got[1]
    return near + flip(far, "x")


def tensor_gather(own):
    size = lax.axis_size("a")
    a = lax.axis_index("a")
    t = lax.axis_index("x") * 2 + lax.axis_index("c")
    pair = jnp.stack([own, flip(own, "x")])
    other = flip(pair, "c")
    pieces = jnp.stack([pair[0], other[0], pair[1], other[1]])
    return jnp.concatenate(
        [lax.dynamic_index_in_dim(pieces, ((a + r) % size) ^ t, 0, False) for r in range(size)], axis=0
    )


def own_half_first(value):
    if lax.axis_size("b") != 2:
        return value
    half = value.shape[-1] // 2
    b = lax.axis_index("b")
    axis = value.ndim - 1
    return jnp.concatenate(
        [
            lax.dynamic_slice_in_dim(value, b * half, half, axis),
            lax.dynamic_slice_in_dim(value, (1 - b) * half, half, axis),
        ],
        axis=axis,
    )


def fetch(shard):
    if lax.axis_size("b") == 2:
        return (shard, flip(shard, "b"))
    return (lax.all_gather(shard, "b", axis=0, tiled=True),)


def dot(left, right, left_dim, right_dim):
    return lax.dot_general(
        left, right, (((left_dim,), (right_dim,)), ((), ())), preferred_element_type=f32
    )


def project_in(rows, pieces):
    total = None
    at = 0
    for piece in pieces:
        part = dot(rows[:, at : at + piece.shape[0]], piece, 1, 0)
        total = part if total is None else total + part
        at += piece.shape[0]
    return total


def project_out(rows, pieces):
    return jnp.concatenate([dot(rows, piece, 1, 1) for piece in pieces], axis=1)


def weight_grad(rows, grads):
    if lax.axis_size("b") == 2:
        half = rows.shape[1] // 2
        sent = dot(rows[:, half:], grads, 0, 0).astype(bf16)
        return dot(rows[:, :half], grads, 0, 0) + flip(sent, "b").astype(f32)
    return lax.psum_scatter(
        dot(rows, grads, 0, 0).astype(bf16), "b", scatter_dimension=0, tiled=True
    ).astype(f32)


def rope_tables(segments, head_size):
    rows = segments.shape[1]
    starts = jnp.sum((segments[:, None, :] < segments[:, :, None]).astype(jnp.int32), axis=2)
    position = (jnp.arange(rows, dtype=jnp.int32)[None] - starts).astype(f32)
    half_size = head_size // 2
    frequency = jnp.power(rope_base, -2.0 * jnp.arange(half_size, dtype=f32) / head_size)
    angles = position[:, :, None] * frequency[None, None, :]
    angles = jnp.concatenate([angles, angles], axis=2)
    return (jnp.cos(angles)[:, :, None, :], jnp.sin(angles)[:, :, None, :])


def visible(segments):
    order = jnp.arange(segments.shape[1], dtype=jnp.int32)
    same = segments[:, :, None] == segments[:, None, :]
    return same & (order[:, None] >= order[None, :])[None]


def apply_rotary(value, cosine, sine):
    half = value.shape[-1] // 2
    turned = jnp.concatenate([-value[..., half:], value[..., :half]], axis=-1)
    return value * cosine + turned * sine


def rotate_back(upstream, cosine, sine):
    scaled = upstream * sine
    half = upstream.shape[-1] // 2
    turned = jnp.concatenate([scaled[..., half:], -scaled[..., :half]], axis=-1)
    return upstream * cosine + turned


def norm_back(upstream, normed, inverse, gain):
    scaled = upstream * gain
    return inverse * (scaled - normed * jnp.mean(scaled * normed, axis=-1, keepdims=True))


def attention_forward(qkv, segments, query_gain, key_gain, kv_heads):
    batch, length = segments.shape
    head = query_gain.shape[0]
    kv_width = kv_heads * head
    heads = (qkv.shape[1] - 2 * kv_width) // head
    query_pre = qkv[:, : heads * head].reshape(batch, length, heads, head)
    key_pre = qkv[:, heads * head : heads * head + kv_width].reshape(batch, length, kv_heads, head)
    value = qkv[:, heads * head + kv_width :].astype(bf16).reshape(batch, length, kv_heads, head)
    cosine, sine = rope_tables(segments, head)
    query_inv = lax.rsqrt(jnp.mean(query_pre * query_pre, axis=3, keepdims=True) + epsilon)
    key_inv = lax.rsqrt(jnp.mean(key_pre * key_pre, axis=3, keepdims=True) + epsilon)
    query_rot = apply_rotary(query_pre * query_inv * query_gain, cosine, sine).astype(bf16)
    query_rot = query_rot.reshape(batch, length, kv_heads, heads // kv_heads, head)
    key_rot = apply_rotary(key_pre * key_inv * key_gain, cosine, sine).astype(bf16)
    allowed = visible(segments)[:, None, None]
    scores = jnp.einsum("bqkgd,bskd->bkgqs", query_rot, key_rot, preferred_element_type=f32)
    scores = jnp.where(allowed, scores * head ** (-0.5), masked_score)
    top = jnp.max(scores, axis=4, keepdims=True)
    exps = jnp.exp(scores - top)
    totals = jnp.sum(exps, axis=4, keepdims=True)
    probs = exps / totals
    probs_low = probs.astype(bf16)
    mixed = jnp.einsum("bkgqs,bskd->bqkgd", probs_low, value, preferred_element_type=f32)
    mixed = mixed.astype(bf16).reshape(batch * length, heads * head)
    return mixed, (query_pre, key_pre, value, query_inv, key_inv, query_rot, key_rot, cosine, sine, probs)


def attention_backward(d_mixed, saved, query_gain, key_gain):
    query_pre, key_pre, value, query_inv, key_inv, query_rot, key_rot, cosine, sine, probs = saved
    batch, length, heads, head = query_pre.shape
    scale = head ** (-0.5)
    d_mixed = d_mixed.astype(bf16).reshape(query_rot.shape)
    d_probs = jnp.einsum("bqkgd,bskd->bkgqs", d_mixed, value, preferred_element_type=f32)
    delta = jnp.sum(probs * d_probs, axis=4, keepdims=True)
    d_scores = (probs * (d_probs - delta)).astype(bf16)
    d_value = jnp.einsum("bkgqs,bqkgd->bskd", probs.astype(bf16), d_mixed, preferred_element_type=f32)
    d_query = jnp.einsum("bkgqs,bskd->bqkgd", d_scores, key_rot, preferred_element_type=f32) * scale
    d_query = d_query.reshape(query_pre.shape)
    d_key = jnp.einsum("bkgqs,bqkgd->bskd", d_scores, query_rot, preferred_element_type=f32) * scale
    query_normed = query_pre * query_inv
    key_normed = key_pre * key_inv
    d_query = rotate_back(d_query, cosine, sine)
    d_key = rotate_back(d_key, cosine, sine)
    query_gain_part = jnp.sum(d_query * query_normed, axis=(0, 1, 2))
    key_gain_part = jnp.sum(d_key * key_normed, axis=(0, 1, 2))
    d_query = norm_back(d_query, query_normed, query_inv, query_gain).astype(bf16)
    d_key = norm_back(d_key, key_normed, key_inv, key_gain).astype(bf16)
    rows = batch * length
    d_qkv = jnp.concatenate(
        [d_query.reshape(rows, -1), d_key.reshape(rows, -1), d_value.astype(bf16).reshape(rows, -1)],
        axis=1,
    )
    return d_qkv, query_gain_part, key_gain_part


def on_device(
    tokens,
    segments,
    w_query,
    key_weight,
    value_weight,
    w_out,
    w_gate,
    w_up,
    w_down,
    attn_gain,
    ffn_gain,
    query_gain,
    key_gain,
    cotangent,
):
    size = lax.axis_size("a")
    width = tokens.shape[1] * size
    head = query_gain.shape[0]
    kv_heads = key_weight.shape[1] // head
    query_width = w_query.shape[1]
    kv_width = key_weight.shape[1]

    x_block = own_half_first(transpose_blocks(tokens)).astype(f32)
    attn_gain = own_half_first(lax.all_gather(attn_gain, ("b", "x", "c"), axis=0, tiled=True))
    ffn_gain = own_half_first(lax.all_gather(ffn_gain, ("b", "x", "c"), axis=0, tiled=True))
    wqkv = fetch(jnp.concatenate([w_query, key_weight, value_weight], axis=1))
    inv_one = lax.rsqrt(ring_sum(jnp.sum(x_block * x_block, axis=1, keepdims=True)) / width + epsilon)
    normed_one = x_block * inv_one
    hidden_one = tensor_gather((normed_one * attn_gain).astype(bf16))
    qkv = ring_scatter(project_in(hidden_one, wqkv))
    mixed, saved = attention_forward(qkv, segments, query_gain, key_gain, kv_heads)
    mixed_rows = ring_gather(mixed)
    wo = fetch(w_out)
    resid = x_block + tensor_scatter(project_out(mixed_rows, wo))
    inv_two = lax.rsqrt(ring_sum(jnp.sum(resid * resid, axis=1, keepdims=True)) / width + epsilon)
    normed_two = resid * inv_two
    hidden_two = tensor_gather((normed_two * ffn_gain).astype(bf16))

    dy_block = own_half_first(transpose_blocks(cotangent))
    dy_rows = tensor_gather(dy_block)
    wd = fetch(w_down)
    d_act = ring_scatter(project_in(dy_rows, wd))
    wg = fetch(w_gate)
    wu = fetch(w_up)
    gate = ring_scatter(project_in(hidden_two, wg))
    up = ring_scatter(project_in(hidden_two, wu))
    sig = jax.nn.sigmoid(gate)
    act = (gate * sig * up).astype(bf16)
    d_gate = (d_act * up * sig * (1.0 + gate * (1.0 - sig))).astype(bf16)
    d_up = (d_act * (gate * sig)).astype(bf16)
    d_gate_rows = ring_gather(d_gate)
    d_up_rows = ring_gather(d_up)
    d_hidden_two = tensor_scatter(project_out(d_gate_rows, wg) + project_out(d_up_rows, wu))
    act_rows = ring_gather(act)
    ffn_out = tensor_scatter(project_out(act_rows, wd))
    block_out = transpose_blocks(own_half_first((resid + ffn_out).astype(bf16)))
    ffn_gain_part = jnp.sum(d_hidden_two * normed_two, axis=0)
    e_two = d_hidden_two * ffn_gain
    stat_two = ring_sum(jnp.sum(e_two * normed_two, axis=1, keepdims=True)) / width
    d_resid = dy_block.astype(f32) + inv_two * (e_two - normed_two * stat_two)
    d_resid_rows = tensor_gather(d_resid.astype(bf16))
    d_mixed = ring_scatter(project_in(d_resid_rows, wo))
    d_qkv, query_part, key_part = attention_backward(d_mixed, saved, query_gain, key_gain)
    d_qkv_rows = ring_gather(d_qkv)
    d_hidden_one = tensor_scatter(project_out(d_qkv_rows, wqkv))
    attn_gain_part = jnp.sum(d_hidden_one * normed_one, axis=0)
    e_one = d_hidden_one * attn_gain
    stat_one = ring_sum(jnp.sum(e_one * normed_one, axis=1, keepdims=True)) / width
    d_tokens = d_resid + inv_one * (e_one - normed_one * stat_one)
    d_tokens = transpose_blocks(own_half_first(d_tokens))

    grad_down = weight_grad(dy_rows, act_rows)
    grad_gate = weight_grad(hidden_two, d_gate_rows)
    grad_up = weight_grad(hidden_two, d_up_rows)
    grad_out = weight_grad(d_resid_rows, mixed_rows)
    grad_qkv = weight_grad(hidden_one, d_qkv_rows)

    head_parts = ring_sum(jnp.stack([query_part, key_part]))
    gains = jnp.concatenate(
        [own_half_first(attn_gain_part), own_half_first(ffn_gain_part), head_parts.reshape(-1)]
    ).reshape(-1, head)
    gains = gains + flip(gains, "c")
    gains = gains + flip(gains, "x")
    gains = gains + flip(gains, "b") if lax.axis_size("b") == 2 else lax.psum(gains, "b")
    chunk = attn_gain_part.shape[0]
    lane = (lax.axis_index("b") * lax.axis_size("x") + lax.axis_index("x")) * lax.axis_size(
        "c"
    ) + lax.axis_index("c")
    part = chunk // (lax.axis_size("b") * size)
    flat = gains.reshape(-1)
    return (
        block_out,
        d_tokens,
        grad_qkv[:, :query_width],
        grad_qkv[:, query_width : query_width + kv_width],
        grad_qkv[:, query_width + kv_width :],
        grad_out,
        grad_gate,
        grad_up,
        grad_down,
        lax.dynamic_slice_in_dim(flat, lane * part, part),
        lax.dynamic_slice_in_dim(flat, chunk + lane * part, part),
        flat[2 * chunk : 2 * chunk + head],
        flat[2 * chunk + head :],
    )


def solution(mesh):
    dp = mesh.shape["dp"]
    tensor = mesh.shape["tensor"]
    split = Mesh(mesh.devices.reshape(tensor, dp // tensor, tensor // 2, 2), ("a", "b", "x", "c"))
    matrix = P(("a", "b"), ("x", "c"))
    vector = P(("a", "b", "x", "c"))
    return jax.shard_map(
        on_device,
        mesh=split,
        in_specs=(matrix, P(("a", "b"), None)) + (matrix,) * 7 + (vector, vector, P(), P(), matrix),
        out_specs=(matrix,) * 9 + (vector, vector, P(), P()),
        check_vma=False,
    )
```

```python
import jax
import jax.numpy as jnp
from jax import lax
from jax.sharding import Mesh
from jax.sharding import PartitionSpec as P

epsilon = 1e-06
rope_base = 1000000.0
masked_score = -1e30
f32 = jnp.float32
bf16 = jnp.bfloat16


def shift(value, axis, step):
    size = lax.axis_size(axis)
    return lax.ppermute(value, axis, [(i, (i + step) % size) for i in range(size)])


def flip(value, axis, mask=1):
    return lax.ppermute(value, axis, [(i, i ^ mask) for i in range(lax.axis_size(axis))])


def transpose_blocks(value):
    size = lax.axis_size("a")
    inner = lax.axis_size("c")
    outer = lax.axis_size("x")
    pairs = []
    for a in range(size):
        for t in range(outer * inner):
            pairs.append((a * size + t, t * size + a))
    return lax.ppermute(value, ("a", "x", "c"), pairs)


def ring_sum(value):
    if lax.axis_size("a") != 4:
        return lax.psum(value, "a")
    value = value + flip(value, "a", 1)
    return value + flip(value, "a", 3)


def line(value, pairs):
    return lax.ppermute(value, "a", pairs)


def ring_scatter(partial, held=()):
    zero, one, two, three = jnp.split(partial, 4, axis=0)
    i = lax.axis_index("a")
    two = two + line(jnp.where(i == 0, three, one), [(0, 1), (3, 2)])
    two, *held = lax.optimization_barrier((two, *held))
    one = one + line(two, [(0, 1), (1, 2)])
    three = three + line(two, [(3, 2), (2, 1)])
    total = zero + line(one, [(0, 1), (1, 2), (2, 3)]) + line(three, [(3, 2), (2, 1), (1, 0)])
    return (total, *held) if held else total


def ring_blocks(own):
    i = lax.axis_index("a")
    before = line(own, [(0, 1), (1, 2), (2, 3)])
    after = line(own, [(3, 2), (2, 1), (1, 0)])
    before_two = line(before, [(1, 2), (2, 3)])
    after_two = line(after, [(2, 1), (1, 0)])
    far = line(jnp.where(i == 2, before_two, after_two), [(2, 3), (1, 0)])
    return [
        own,
        jnp.where(i == 3, far, after),
        jnp.where(i < 2, after_two, before_two),
        jnp.where(i == 0, far, before),
    ]


def ring_gather(own, axis=0):
    return jnp.concatenate(ring_blocks(own), axis=axis)


def column_block(value, r):
    size = lax.axis_size("a")
    width = value.shape[1] // size
    return lax.dynamic_slice_in_dim(value, ((lax.axis_index("a") + r) % size) * width, width, 1)


def ring_columns(value):
    return jnp.concatenate([column_block(value, r) for r in range(4)], axis=1)


def plain_columns(value):
    twice = 2 * lax.axis_index("a")
    return jnp.concatenate([column_block(value, r - twice) for r in range(4)], axis=1)


def swap_columns(shards):
    def blocks(r):
        return jnp.concatenate([column_block(shard, r) for shard in shards], axis=1)

    return [blocks(0)] + [shift(blocks(4 - r), "a", 4 - r) for r in (1, 2, 3)]


def together(*values):
    return lax.optimization_barrier(values)


def gather_all(own):
    pieces = ring_blocks(jnp.concatenate([own, flip(own, "x")], axis=0))
    return [jnp.concatenate([piece, flip(piece, "c")], axis=0) for piece in pieces]


def flip_scatter(partial):
    blocks = partial.reshape(2, 2, partial.shape[0] // 4, partial.shape[1])
    pair = blocks[0] + flip(blocks[1], "c")
    return pair[0] + flip(pair[1], "x")


def tensor_scatter(partial):
    size = lax.axis_size("a")
    a = lax.axis_index("a")
    x = lax.axis_index("x")
    c = lax.axis_index("c")
    rows = partial.shape[0] // size

    def block(t):
        return lax.dynamic_slice_in_dim(partial, ((t - a) % size) * rows, rows)

    send = jnp.stack([block(2 * (1 - x) + 1 - c), block(2 * x + 1 - c)])
    got = flip(send, "c")
    far = block(2 * (1 - x) + c) + got[0]
    near = block(2 * x + c) + got[1]
    return near + flip(far, "x")


def tensor_gather(own):
    size = lax.axis_size("a")
    a = lax.axis_index("a")
    t = lax.axis_index("x") * 2 + lax.axis_index("c")
    pair = jnp.stack([own, flip(own, "x")])
    other = flip(pair, "c")
    pieces = jnp.stack([pair[0], other[0], pair[1], other[1]])
    return jnp.concatenate(
        [lax.dynamic_index_in_dim(pieces, ((a + r) % size) ^ t, 0, False) for r in range(size)], axis=0
    )


def chunk_gains(value):
    if lax.axis_size("b") != 2:
        return lax.all_gather(value, ("b", "x", "c"), axis=0, tiled=False)
    lane = (lax.axis_index("b") * 2 + lax.axis_index("x")) * 2 + lax.axis_index("c")
    total = lax.dynamic_update_slice_in_dim(jnp.zeros((8,) + value.shape, f32), value[None], lane, 0)
    for axis in ("c", "x", "b"):
        total = total + flip(total, axis)
    return total


def fetch(shard):
    return lax.all_gather(shard, "b", axis=0, tiled=True)


def dot(left, right, left_dim, right_dim):
    return lax.dot_general(
        left, right, (((left_dim,), (right_dim,)), ((), ())), preferred_element_type=f32
    )


def project_in(rows, weight):
    return dot(rows, weight, 1, 0)


def project_out(rows, weight):
    return dot(rows, weight, 1, 1)


def project_all(pieces, weights):
    total = None
    for piece, weight in zip(pieces, weights):
        part = project_in(piece, weight)
        total = part if total is None else total + part
    return total


def project_blocks(blocks, weight, total=None):
    width = blocks[0].shape[1]
    for r, block in enumerate(blocks):
        part = project_out(block, weight[:, r * width : (r + 1) * width])
        total = part if total is None else total + part
    return total


def weight_partial(rows, grads):
    return dot(rows, grads, 0, 0).astype(bf16)


def pair_scatter(partial):
    return lax.psum_scatter(partial, "b", scatter_dimension=0, tiled=True).astype(f32)


def weight_grad(rows, grads):
    return pair_scatter(weight_partial(rows, grads))


def rope_tables(segments, head_size):
    rows = segments.shape[1]
    starts = jnp.sum((segments[:, None, :] < segments[:, :, None]).astype(jnp.int32), axis=2)
    position = (jnp.arange(rows, dtype=jnp.int32)[None] - starts).astype(f32)
    half_size = head_size // 2
    frequency = jnp.power(rope_base, -2.0 * jnp.arange(half_size, dtype=f32) / head_size)
    angles = position[:, :, None] * frequency[None, None, :]
    angles = jnp.concatenate([angles, angles], axis=2)
    return (jnp.cos(angles)[:, :, None, :], jnp.sin(angles)[:, :, None, :])


def visible(segments):
    order = jnp.arange(segments.shape[1], dtype=jnp.int32)
    same = segments[:, :, None] == segments[:, None, :]
    return same & (order[:, None] >= order[None, :])[None]


def apply_rotary(value, cosine, sine):
    half = value.shape[-1] // 2
    turned = jnp.concatenate([-value[..., half:], value[..., :half]], axis=-1)
    return value * cosine + turned * sine


def rotate_back(upstream, cosine, sine):
    scaled = upstream * sine
    half = upstream.shape[-1] // 2
    turned = jnp.concatenate([scaled[..., half:], -scaled[..., :half]], axis=-1)
    return upstream * cosine + turned


def norm_back(upstream, normed, inverse, gain):
    scaled = upstream * gain
    return inverse * (scaled - normed * jnp.mean(scaled * normed, axis=-1, keepdims=True))


def attention_forward(qkv, segments, query_gain, key_gain, kv_heads):
    batch, length = segments.shape
    head = query_gain.shape[0]
    kv_width = kv_heads * head
    heads = (qkv.shape[1] - 2 * kv_width) // head
    query_pre = qkv[:, : heads * head].reshape(batch, length, heads, head)
    key_pre = qkv[:, heads * head : heads * head + kv_width].reshape(batch, length, kv_heads, head)
    value = qkv[:, heads * head + kv_width :].astype(bf16).reshape(batch, length, kv_heads, head)
    cosine, sine = rope_tables(segments, head)
    query_inv = lax.rsqrt(jnp.mean(query_pre * query_pre, axis=3, keepdims=True) + epsilon)
    key_inv = lax.rsqrt(jnp.mean(key_pre * key_pre, axis=3, keepdims=True) + epsilon)
    query_rot = apply_rotary(query_pre * query_inv * query_gain, cosine, sine).astype(bf16)
    query_rot = query_rot.reshape(batch, length, kv_heads, heads // kv_heads, head)
    key_rot = apply_rotary(key_pre * key_inv * key_gain, cosine, sine).astype(bf16)
    allowed = visible(segments)[:, None, None]
    scores = jnp.einsum("bqkgd,bskd->bkgqs", query_rot, key_rot, preferred_element_type=f32)
    scores = jnp.where(allowed, scores * head ** (-0.5), masked_score)
    top = jnp.max(scores, axis=4, keepdims=True)
    exps = jnp.exp(scores - top)
    totals = jnp.sum(exps, axis=4, keepdims=True)
    probs = exps / totals
    probs_low = probs.astype(bf16)
    mixed = jnp.einsum("bkgqs,bskd->bqkgd", probs_low, value, preferred_element_type=f32)
    mixed = mixed.astype(bf16).reshape(batch * length, heads * head)
    return mixed, (query_pre, key_pre, value, query_inv, key_inv, query_rot, key_rot, cosine, sine, probs)


def attention_backward(d_mixed, saved, query_gain, key_gain):
    query_pre, key_pre, value, query_inv, key_inv, query_rot, key_rot, cosine, sine, probs = saved
    batch, length, heads, head = query_pre.shape
    scale = head ** (-0.5)
    d_mixed = d_mixed.astype(bf16).reshape(query_rot.shape)
    d_probs = jnp.einsum("bqkgd,bskd->bkgqs", d_mixed, value, preferred_element_type=f32)
    delta = jnp.sum(probs * d_probs, axis=4, keepdims=True)
    d_scores = (probs * (d_probs - delta)).astype(bf16)
    d_value = jnp.einsum("bkgqs,bqkgd->bskd", probs.astype(bf16), d_mixed, preferred_element_type=f32)
    d_query = jnp.einsum("bkgqs,bskd->bqkgd", d_scores, key_rot, preferred_element_type=f32) * scale
    d_query = d_query.reshape(query_pre.shape)
    d_key = jnp.einsum("bkgqs,bqkgd->bskd", d_scores, query_rot, preferred_element_type=f32) * scale
    query_normed = query_pre * query_inv
    key_normed = key_pre * key_inv
    d_query = rotate_back(d_query, cosine, sine)
    d_key = rotate_back(d_key, cosine, sine)
    query_gain_part = jnp.sum(d_query * query_normed, axis=(0, 1, 2))
    key_gain_part = jnp.sum(d_key * key_normed, axis=(0, 1, 2))
    d_query = norm_back(d_query, query_normed, query_inv, query_gain).astype(bf16)
    d_key = norm_back(d_key, key_normed, key_inv, key_gain).astype(bf16)
    rows = batch * length
    d_qkv = jnp.concatenate(
        [d_query.reshape(rows, -1), d_key.reshape(rows, -1), d_value.astype(bf16).reshape(rows, -1)],
        axis=1,
    )
    return d_qkv, query_gain_part, key_gain_part


def on_device(
    tokens,
    segments,
    w_query,
    key_weight,
    value_weight,
    w_out,
    w_gate,
    w_up,
    w_down,
    attn_gain,
    ffn_gain,
    query_gain,
    key_gain,
    cotangent,
):
    size = lax.axis_size("a")
    width = tokens.shape[1] * size
    head = query_gain.shape[0]
    kv_heads = key_weight.shape[1] // head
    query_width = w_query.shape[1]
    kv_width = key_weight.shape[1]

    x_block = transpose_blocks(tokens).astype(f32)
    dy_block = transpose_blocks(cotangent)
    gains = chunk_gains(jnp.stack([attn_gain, ffn_gain]))
    attn_gain = gains[:, 0].reshape(-1)
    ffn_gain = gains[:, 1].reshape(-1)
    wqkv = fetch(jnp.concatenate([w_query, key_weight, value_weight], axis=1))
    inv_one = lax.rsqrt(ring_sum(jnp.sum(x_block * x_block, axis=1, keepdims=True)) / width + epsilon)
    normed_one = x_block * inv_one
    hidden_block, dy_block = together((normed_one * attn_gain).astype(bf16), dy_block)
    columns = swap_columns([w_gate, w_up])
    hidden_one = tensor_gather(hidden_block)
    qkv, *columns = ring_scatter(project_in(hidden_one, wqkv), tuple(columns))
    wo = fetch(w_out)
    columns = [fetch(piece) for piece in columns]
    qkv, down = together(qkv, w_down)
    down = swap_columns([down])
    mixed, saved = attention_forward(qkv, segments, query_gain, key_gain, kv_heads)
    mixed, *down = together(mixed, *down)
    down = [fetch(piece) for piece in down]
    mixed_rows, dy_block = together(ring_gather(mixed), dy_block)
    dy_pieces = gather_all(dy_block)
    resid = x_block + tensor_scatter(project_out(mixed_rows, wo))
    inv_two = lax.rsqrt(ring_sum(jnp.sum(resid * resid, axis=1, keepdims=True)) / width + epsilon)
    normed_two = resid * inv_two
    hidden_block, *dy_pieces = together((normed_two * ffn_gain).astype(bf16), *dy_pieces)
    dy_rows = dy_pieces[0]
    hidden_pieces = gather_all(hidden_block)
    hidden_two = hidden_pieces[0]

    d_act = project_all(dy_pieces, down)
    gate, up = jnp.split(project_all(hidden_pieces, columns), 2, axis=1)
    wg = fetch(ring_columns(w_gate))
    wu = fetch(ring_columns(w_up))
    wd = fetch(ring_columns(w_down))
    sig = jax.nn.sigmoid(gate)
    act = (gate * sig * up).astype(bf16)
    d_gate = (d_act * up * sig * (1.0 + gate * (1.0 - sig))).astype(bf16)
    d_up = (d_act * (gate * sig)).astype(bf16)
    d_gate = ring_blocks(d_gate)
    d_up = ring_blocks(d_up)
    d_hidden_two = flip_scatter(project_blocks(d_up, wu, project_blocks(d_gate, wg)))
    *d_up, act = together(*d_up, act)
    act_rows = ring_gather(act, 1)
    ffn_gain_part = jnp.sum(d_hidden_two * normed_two, axis=0)
    e_two = d_hidden_two * ffn_gain
    stat_two = ring_sum(jnp.sum(e_two * normed_two, axis=1, keepdims=True)) / width
    d_resid = dy_block.astype(f32) + inv_two * (e_two - normed_two * stat_two)
    d_resid_rows, act_rows = together(tensor_gather(d_resid.astype(bf16)), act_rows)
    d_mixed = ring_scatter(project_in(d_resid_rows, wo))
    grad_down = weight_partial(dy_rows, act_rows)
    ffn_out = project_out(act_rows, wd)
    d_mixed, grad_down, ffn_out = together(d_mixed, grad_down, ffn_out)
    grad_down = pair_scatter(grad_down)
    ffn_out = flip_scatter(ffn_out)
    block_out = transpose_blocks((resid + ffn_out).astype(bf16))
    d_qkv, query_part, key_part = attention_backward(d_mixed, saved, query_gain, key_gain)
    d_qkv_rows = ring_gather(d_qkv)
    d_hidden_one = tensor_scatter(project_out(d_qkv_rows, wqkv))
    grad_gate = plain_columns(weight_grad(hidden_two, jnp.concatenate(d_gate, axis=1)))
    grad_up = plain_columns(weight_grad(hidden_two, jnp.concatenate(d_up, axis=1)))
    d_hidden_one, grad_gate, grad_up = together(d_hidden_one, grad_gate, grad_up)
    attn_gain_part = jnp.sum(d_hidden_one * normed_one, axis=0)
    e_one = d_hidden_one * attn_gain
    stat_one = ring_sum(jnp.sum(e_one * normed_one, axis=1, keepdims=True)) / width
    d_tokens = d_resid + inv_one * (e_one - normed_one * stat_one)
    d_tokens = transpose_blocks(d_tokens)
    grad_out = weight_grad(d_resid_rows, mixed_rows)
    grad_qkv = weight_grad(hidden_one, d_qkv_rows)

    head_parts = ring_sum(jnp.stack([query_part, key_part]))
    gains = jnp.concatenate(
        [attn_gain_part, ffn_gain_part, head_parts.reshape(-1)]
    ).reshape(-1, head)
    gains = gains + flip(gains, "c")
    gains = gains + flip(gains, "x")
    gains = gains + flip(gains, "b") if lax.axis_size("b") == 2 else lax.psum(gains, "b")
    chunk = attn_gain_part.shape[0]
    lane = (lax.axis_index("b") * lax.axis_size("x") + lax.axis_index("x")) * lax.axis_size(
        "c"
    ) + lax.axis_index("c")
    part = chunk // (lax.axis_size("b") * size)
    flat = gains.reshape(-1)
    return (
        block_out,
        d_tokens,
        grad_qkv[:, :query_width],
        grad_qkv[:, query_width : query_width + kv_width],
        grad_qkv[:, query_width + kv_width :],
        grad_out,
        grad_gate,
        grad_up,
        plain_columns(grad_down),
        lax.dynamic_slice_in_dim(flat, lane * part, part),
        lax.dynamic_slice_in_dim(flat, chunk + lane * part, part),
        flat[2 * chunk : 2 * chunk + head],
        flat[2 * chunk + head :],
    )


def solution(mesh):
    dp = mesh.shape["dp"]
    tensor = mesh.shape["tensor"]
    split = Mesh(mesh.devices.reshape(tensor, dp // tensor, tensor // 2, 2), ("a", "b", "x", "c"))
    matrix = P(("a", "b"), ("x", "c"))
    vector = P(("a", "b", "x", "c"))
    return jax.shard_map(
        on_device,
        mesh=split,
        in_specs=(matrix, P(("a", "b"), None)) + (matrix,) * 7 + (vector, vector, P(), P(), matrix),
        out_specs=(matrix,) * 9 + (vector, vector, P(), P()),
        check_vma=False,
    )
```

```python
import jax
import jax.numpy as jnp
from jax import lax
from jax.sharding import Mesh
from jax.sharding import PartitionSpec as P

epsilon = 1e-06
rope_base = 1000000.0
masked_score = -1e30
f32 = jnp.float32
bf16 = jnp.bfloat16


def shift(value, axis, step):
    size = lax.axis_size(axis)
    return lax.ppermute(value, axis, [(i, (i + step) % size) for i in range(size)])


def flip(value, axis, mask=1):
    return lax.ppermute(value, axis, [(i, i ^ mask) for i in range(lax.axis_size(axis))])


def transpose_blocks(value):
    size = lax.axis_size("a")
    inner = lax.axis_size("c")
    outer = lax.axis_size("x")
    pairs = []
    for a in range(size):
        for t in range(outer * inner):
            pairs.append((a * size + t, t * size + a))
    return lax.ppermute(value, ("a", "x", "c"), pairs)


def ring_sum(value):
    if lax.axis_size("a") != 4:
        return lax.psum(value, "a")
    value = value + flip(value, "a", 1)
    return value + flip(value, "a", 3)


def line(value, pairs):
    return lax.ppermute(value, "a", pairs)


def ring_scatter(partial, held=(), held_two=()):
    return ring_add(jnp.split(partial, 4, axis=0), held, held_two)


def ring_add(blocks, held=(), held_two=()):
    zero, one, two, three = blocks
    i = lax.axis_index("a")
    two = two + line(jnp.where(i == 0, three, one), [(0, 1), (3, 2)])
    two, *held = lax.optimization_barrier((two, *held))
    one = one + line(two, [(0, 1), (1, 2)])
    three = three + line(two, [(3, 2), (2, 1)])
    one, three, *held_two = lax.optimization_barrier((one, three, *held_two))
    total = zero + line(one, [(0, 1), (1, 2), (2, 3)]) + line(three, [(3, 2), (2, 1), (1, 0)])
    return (total, *held, *held_two) if held or held_two else total


def ring_first(own):
    return line(own, [(0, 1), (1, 2), (2, 3)]), line(own, [(3, 2), (2, 1), (1, 0)])


def ring_second(before, behind):
    return line(before, [(1, 2), (2, 3)]), line(behind, [(2, 1), (1, 0)])


def ring_third(before_two, behind_two):
    i = lax.axis_index("a")
    return line(jnp.where(i == 2, before_two, behind_two), [(2, 3), (1, 0)])


def ring_order(own, before, behind, before_two, behind_two, far):
    i = lax.axis_index("a")
    return [
        own,
        jnp.where(i == 3, far, behind),
        jnp.where(i < 2, behind_two, before_two),
        jnp.where(i == 0, far, before),
    ]


def ring_blocks(own):
    first = ring_first(own)
    second = ring_second(*first)
    return ring_order(own, *first, *second, ring_third(*second))


def ring_gather(own, axis=0):
    return jnp.concatenate(ring_blocks(own), axis=axis)


def column_block(value, r):
    size = lax.axis_size("a")
    width = value.shape[1] // size
    return lax.dynamic_slice_in_dim(value, ((lax.axis_index("a") + r) % size) * width, width, 1)


def ring_columns(*values):
    return jnp.concatenate([column_block(value, r) for r in range(4) for value in values], axis=1)


def plain_columns(value, which=0, count=1):
    size = lax.axis_size("a")
    width = value.shape[1] // (size * count)
    a = lax.axis_index("a")
    blocks = []
    for j in range(size):
        at = ((j - a) % size) * count + which
        blocks.append(lax.dynamic_slice_in_dim(value, at * width, width, 1))
    return jnp.concatenate(blocks, axis=1).astype(f32)


def swapped(shards, r):
    blocks = [column_block(shard, (4 - r) % 4) for shard in shards]
    blocks = jnp.concatenate(blocks, axis=1) if len(blocks) > 1 else blocks[0]
    return shift(blocks, "a", 4 - r) if r else blocks


def together(*values):
    return lax.optimization_barrier(values)


def gather_all(own):
    i = lax.axis_index("a")

    def spread(block):
        pair = jnp.concatenate([block, flip(block, "x")], axis=0)
        return jnp.concatenate([pair, flip(pair, "c")], axis=0)

    first = ring_first(own)
    second = ring_second(*first)
    far = ring_third(*second)
    two = jnp.where(i < 2, second[1], second[0])
    return [spread(block) for block in (own, first[1], two, first[0], far)]


def ring_pieces(pieces):
    i = lax.axis_index("a")
    own, one, two, three, far = pieces
    return [own, jnp.where(i == 3, far, one), two, jnp.where(i == 0, far, three)]


def flip_half(partial):
    blocks = partial.reshape(2, 2, partial.shape[0] // 4, partial.shape[1])
    return blocks[0] + flip(blocks[1], "c")


def flip_rest(pair):
    return pair[0] + flip(pair[1], "x")


def tensor_scatter(partial):
    size = lax.axis_size("a")
    a = lax.axis_index("a")
    x = lax.axis_index("x")
    c = lax.axis_index("c")
    rows = partial.shape[0] // size

    def block(t):
        return lax.dynamic_slice_in_dim(partial, ((t - a) % size) * rows, rows)

    send = jnp.stack([block(2 * (1 - x) + 1 - c), block(2 * x + 1 - c)])
    got = flip(send, "c")
    far = block(2 * (1 - x) + c) + got[0]
    near = block(2 * x + c) + got[1]
    return near + flip(far, "x")


def tensor_gather(own):
    size = lax.axis_size("a")
    a = lax.axis_index("a")
    t = lax.axis_index("x") * 2 + lax.axis_index("c")
    pair = jnp.stack([own, flip(own, "x")])
    other = flip(pair, "c")
    pieces = jnp.stack([pair[0], other[0], pair[1], other[1]])
    return jnp.concatenate(
        [lax.dynamic_index_in_dim(pieces, ((a + r) % size) ^ t, 0, False) for r in range(size)], axis=0
    )


def chunk_gains(value):
    if lax.axis_size("b") != 2:
        return lax.all_gather(value, ("b", "x", "c"), axis=0, tiled=False)
    lane = (lax.axis_index("b") * 2 + lax.axis_index("x")) * 2 + lax.axis_index("c")
    total = lax.dynamic_update_slice_in_dim(jnp.zeros((8,) + value.shape, f32), value[None], lane, 0)
    for axis in ("c", "x", "b"):
        total = total + flip(total, axis)
    return total


def fetch(shard):
    return lax.all_gather(shard, "b", axis=0, tiled=True)


def dot(left, right, left_dim, right_dim):
    return lax.dot_general(
        left, right, (((left_dim,), (right_dim,)), ((), ())), preferred_element_type=f32
    )


def project_in(rows, weight):
    return dot(rows, weight, 1, 0)


def project_out(rows, weight):
    return dot(rows, weight, 1, 1)


def project_all(pieces, weights):
    total = project_in(pieces[0], weights[0])
    for r in (1, 3, 2):
        total = total + project_in(pieces[r], weights[r])
    weight = jnp.where(lax.axis_index("a") == 3, weights[1], weights[3])
    total, weight, far = together(total, weight, pieces[4])
    return total + project_in(far, weight)


def weight_partial(rows, grads):
    return dot(rows, grads, 0, 0).astype(bf16)


def pair_scatter(partial):
    return lax.psum_scatter(partial, "b", scatter_dimension=0, tiled=True)


def weight_grad(rows, grads):
    return pair_scatter(weight_partial(rows, grads)).astype(f32)


def rope_tables(segments, head_size):
    rows = segments.shape[1]
    starts = jnp.sum((segments[:, None, :] < segments[:, :, None]).astype(jnp.int32), axis=2)
    position = (jnp.arange(rows, dtype=jnp.int32)[None] - starts).astype(f32)
    half_size = head_size // 2
    frequency = jnp.power(rope_base, -2.0 * jnp.arange(half_size, dtype=f32) / head_size)
    angles = position[:, :, None] * frequency[None, None, :]
    angles = jnp.concatenate([angles, angles], axis=2)
    return (jnp.cos(angles)[:, :, None, :], jnp.sin(angles)[:, :, None, :])


def visible(segments):
    order = jnp.arange(segments.shape[1], dtype=jnp.int32)
    same = segments[:, :, None] == segments[:, None, :]
    return same & (order[:, None] >= order[None, :])[None]


def apply_rotary(value, cosine, sine):
    half = value.shape[-1] // 2
    turned = jnp.concatenate([-value[..., half:], value[..., :half]], axis=-1)
    return value * cosine + turned * sine


def rotate_back(upstream, cosine, sine):
    scaled = upstream * sine
    half = upstream.shape[-1] // 2
    turned = jnp.concatenate([scaled[..., half:], -scaled[..., :half]], axis=-1)
    return upstream * cosine + turned


def norm_back(upstream, normed, inverse, gain):
    scaled = upstream * gain
    return inverse * (scaled - normed * jnp.mean(scaled * normed, axis=-1, keepdims=True))


def attention_forward(qkv, segments, query_gain, key_gain, kv_heads):
    batch, length = segments.shape
    head = query_gain.shape[0]
    kv_width = kv_heads * head
    heads = (qkv.shape[1] - 2 * kv_width) // head
    query_pre = qkv[:, : heads * head].reshape(batch, length, heads, head)
    key_pre = qkv[:, heads * head : heads * head + kv_width].reshape(batch, length, kv_heads, head)
    value = qkv[:, heads * head + kv_width :].astype(bf16).reshape(batch, length, kv_heads, head)
    cosine, sine = rope_tables(segments, head)
    query_inv = lax.rsqrt(jnp.mean(query_pre * query_pre, axis=3, keepdims=True) + epsilon)
    key_inv = lax.rsqrt(jnp.mean(key_pre * key_pre, axis=3, keepdims=True) + epsilon)
    query_rot = apply_rotary(query_pre * query_inv * query_gain, cosine, sine).astype(bf16)
    query_rot = query_rot.reshape(batch, length, kv_heads, heads // kv_heads, head)
    key_rot = apply_rotary(key_pre * key_inv * key_gain, cosine, sine).astype(bf16)
    allowed = visible(segments)[:, None, None]
    scores = jnp.einsum("bqkgd,bskd->bkgqs", query_rot, key_rot, preferred_element_type=f32)
    scores = jnp.where(allowed, scores * head ** (-0.5), masked_score)
    top = jnp.max(scores, axis=4, keepdims=True)
    exps = jnp.exp(scores - top)
    totals = jnp.sum(exps, axis=4, keepdims=True)
    probs = exps / totals
    probs_low = probs.astype(bf16)
    mixed = jnp.einsum("bkgqs,bskd->bqkgd", probs_low, value, preferred_element_type=f32)
    mixed = mixed.astype(bf16).reshape(batch * length, heads * head)
    return mixed, (query_pre, key_pre, value, query_inv, key_inv, query_rot, key_rot, cosine, sine, probs)


def attention_backward(d_mixed, saved, query_gain, key_gain):
    query_pre, key_pre, value, query_inv, key_inv, query_rot, key_rot, cosine, sine, probs = saved
    batch, length, heads, head = query_pre.shape
    scale = head ** (-0.5)
    d_mixed = d_mixed.astype(bf16).reshape(query_rot.shape)
    d_probs = jnp.einsum("bqkgd,bskd->bkgqs", d_mixed, value, preferred_element_type=f32)
    delta = jnp.sum(probs * d_probs, axis=4, keepdims=True)
    d_scores = (probs * (d_probs - delta)).astype(bf16)
    d_value = jnp.einsum("bkgqs,bqkgd->bskd", probs.astype(bf16), d_mixed, preferred_element_type=f32)
    d_query = jnp.einsum("bkgqs,bskd->bqkgd", d_scores, key_rot, preferred_element_type=f32) * scale
    d_query = d_query.reshape(query_pre.shape)
    d_key = jnp.einsum("bkgqs,bqkgd->bskd", d_scores, query_rot, preferred_element_type=f32) * scale
    query_normed = query_pre * query_inv
    key_normed = key_pre * key_inv
    d_query = rotate_back(d_query, cosine, sine)
    d_key = rotate_back(d_key, cosine, sine)
    query_gain_part = jnp.sum(d_query * query_normed, axis=(0, 1, 2))
    key_gain_part = jnp.sum(d_key * key_normed, axis=(0, 1, 2))
    d_query = norm_back(d_query, query_normed, query_inv, query_gain).astype(bf16)
    d_key = norm_back(d_key, key_normed, key_inv, key_gain).astype(bf16)
    rows = batch * length
    d_qkv = jnp.concatenate(
        [d_query.reshape(rows, -1), d_key.reshape(rows, -1), d_value.astype(bf16).reshape(rows, -1)],
        axis=1,
    )
    return d_qkv, query_gain_part, key_gain_part


def on_device(
    tokens,
    segments,
    w_query,
    key_weight,
    value_weight,
    w_out,
    w_gate,
    w_up,
    w_down,
    attn_gain,
    ffn_gain,
    query_gain,
    key_gain,
    cotangent,
):
    size = lax.axis_size("a")
    width = tokens.shape[1] * size
    head = query_gain.shape[0]
    kv_heads = key_weight.shape[1] // head
    query_width = w_query.shape[1]
    kv_width = key_weight.shape[1]

    x_block = transpose_blocks(tokens).astype(f32)
    wqkv = jnp.concatenate([w_query, key_weight, value_weight], axis=1)
    gains, wqkv = together(jnp.stack([attn_gain, ffn_gain]), wqkv)
    wqkv = fetch(wqkv)
    gains = chunk_gains(gains)
    attn_gain = gains[:, 0].reshape(-1)
    ffn_gain = gains[:, 1].reshape(-1)
    inv_one = lax.rsqrt(ring_sum(jnp.sum(x_block * x_block, axis=1, keepdims=True)) / width + epsilon)
    normed_one = x_block * inv_one
    hidden_block, gate_shard, up_shard = together(
        (normed_one * attn_gain).astype(bf16), w_gate, w_up
    )
    near = [swapped([gate_shard, up_shard], r) for r in (1, 3)]
    hidden_one = tensor_gather(hidden_block)
    qkv, *near = ring_scatter(project_in(hidden_one, wqkv), near)
    wo = fetch(w_out)
    zero, one, three = [fetch(piece) for piece in (swapped([w_gate, w_up], 0), *near)]
    qkv, down_shard = together(qkv, w_down)
    down = [swapped([down_shard], r) for r in range(4)]
    mixed, saved = attention_forward(qkv, segments, query_gain, key_gain, kv_heads)
    mixed, zero, one, three, dy_block, *down = together(mixed, zero, one, three, cotangent, *down)
    dy_block = transpose_blocks(dy_block)
    dy_pieces = gather_all(dy_block)
    down = [fetch(piece) for piece in down]
    mixed_rows, gate_shard, up_shard = together(ring_gather(mixed), w_gate, w_up)
    opposite = swapped([gate_shard, up_shard], 2)
    resid = x_block + tensor_scatter(project_out(mixed_rows, wo))
    inv_two = lax.rsqrt(ring_sum(jnp.sum(resid * resid, axis=1, keepdims=True)) / width + epsilon)
    normed_two = resid * inv_two
    values = together((normed_two * ffn_gain).astype(bf16), opposite, *down, *dy_pieces)
    hidden_block, opposite, down, dy_pieces = values[0], values[1], values[2:6], values[6:]
    dy_rows = dy_pieces[0]
    two = fetch(opposite)
    columns = [zero, one, two, three]
    hidden_pieces = gather_all(hidden_block)
    d_act = project_all(dy_pieces, down)
    gate, up = jnp.split(project_all(hidden_pieces, columns), 2, axis=1)
    hidden_pieces = ring_pieces(hidden_pieces)
    wd = fetch(ring_columns(w_down))
    sig = jax.nn.sigmoid(gate)
    act = (gate * sig * up).astype(bf16)
    d_gate = (d_act * up * sig * (1.0 + gate * (1.0 - sig))).astype(bf16)
    d_up = (d_act * (gate * sig)).astype(bf16)
    d_gate_up = jnp.concatenate([d_gate, d_up], axis=1)
    parts = {r: project_out(d_gate_up, columns[r]) for r in (3, 1)}
    parts[3], parts[1], d_gate_up = together(parts[3], parts[1], d_gate_up)
    next_grad = weight_partial(hidden_pieces[1], d_gate_up)
    d_gate_up, next_grad = together(d_gate_up, next_grad)
    next_grad = shift(pair_scatter(next_grad), "a", 1)
    parts.update({r: project_out(d_gate_up, columns[r]) for r in (2, 0)})
    parts = {r: flip_half(parts[r]) for r in (3, 1, 2, 0)}
    parts[3], *act_first = together(parts[3], *ring_first(act))
    act_second = ring_second(*act_first)
    parts = {r: flip_rest(parts[r]) for r in (3, 1, 2, 0)}
    parts[3], parts[1], next_grad, *act_second = together(
        parts[3], parts[1], next_grad, *act_second
    )
    d_hidden_two, *grads = together(
        ring_add([parts[r] for r in range(4)]),
        *[weight_partial(hidden_pieces[r], d_gate_up) for r in (3, 2, 0)],
    )
    last_grad, far_grad, own_grad = [pair_scatter(grad) for grad in grads]
    last_grad = shift(last_grad, "a", 3)
    ffn_gain_part = jnp.sum(d_hidden_two * normed_two, axis=0)
    e_two = d_hidden_two * ffn_gain
    stat_two = ring_sum(jnp.sum(e_two * normed_two, axis=1, keepdims=True)) / width
    d_resid = dy_block.astype(f32) + inv_two * (e_two - normed_two * stat_two)
    d_resid_rows = tensor_gather(d_resid.astype(bf16))
    d_mixed, last_grad = together(project_in(d_resid_rows, wo), last_grad)
    d_mixed, far_grad, own_grad, *act_second = together(
        ring_scatter(d_mixed), far_grad, own_grad, *act_second
    )
    act_third = ring_third(*act_second)
    d_qkv, query_part, key_part = attention_backward(d_mixed, saved, query_gain, key_gain)
    d_qkv, act_third = together(d_qkv, act_third)
    act_rows = jnp.concatenate(ring_order(act, *act_first, *act_second, act_third), axis=1)
    d_qkv_rows, head_parts, grad_down, ffn_out, grad_out = together(
        ring_gather(d_qkv),
        ring_sum(jnp.stack([query_part, key_part])),
        weight_partial(dy_rows, act_rows),
        project_out(act_rows, wd),
        weight_partial(d_resid_rows, mixed_rows),
    )
    grad_down = pair_scatter(grad_down)
    grad_out = pair_scatter(grad_out).astype(f32)
    block_out = transpose_blocks((resid + flip_rest(flip_half(ffn_out))).astype(bf16))
    d_qkv_rows, far_grad = together(d_qkv_rows, far_grad)
    d_hidden_one, far_grad = together(
        tensor_scatter(project_out(d_qkv_rows, wqkv)), shift(far_grad, "a", 2)
    )
    attn_gain_part = jnp.sum(d_hidden_one * normed_one, axis=0)
    e_one = d_hidden_one * attn_gain
    stat_one = ring_sum(jnp.sum(e_one * normed_one, axis=1, keepdims=True)) / width
    d_tokens = d_resid + inv_one * (e_one - normed_one * stat_one)
    d_tokens = transpose_blocks(d_tokens)
    grad_gate_up = jnp.concatenate([own_grad, last_grad, far_grad, next_grad], axis=1)
    grad_gate = plain_columns(grad_gate_up, 0, 2)
    grad_up = plain_columns(grad_gate_up, 1, 2)
    grad_down = plain_columns(grad_down)
    grad_qkv = weight_grad(hidden_one, d_qkv_rows)

    gains = jnp.concatenate(
        [attn_gain_part, ffn_gain_part, head_parts.reshape(-1)]
    ).reshape(-1, head)
    gains = gains + flip(gains, "c")
    gains = gains + flip(gains, "x")
    gains = gains + flip(gains, "b") if lax.axis_size("b") == 2 else lax.psum(gains, "b")
    chunk = attn_gain_part.shape[0]
    lane = (lax.axis_index("b") * lax.axis_size("x") + lax.axis_index("x")) * lax.axis_size(
        "c"
    ) + lax.axis_index("c")
    part = chunk // (lax.axis_size("b") * size)
    flat = gains.reshape(-1)
    return (
        block_out,
        d_tokens,
        grad_qkv[:, :query_width],
        grad_qkv[:, query_width : query_width + kv_width],
        grad_qkv[:, query_width + kv_width :],
        grad_out,
        grad_gate,
        grad_up,
        grad_down,
        lax.dynamic_slice_in_dim(flat, lane * part, part),
        lax.dynamic_slice_in_dim(flat, chunk + lane * part, part),
        flat[2 * chunk : 2 * chunk + head],
        flat[2 * chunk + head :],
    )


def solution(mesh):
    dp = mesh.shape["dp"]
    tensor = mesh.shape["tensor"]
    split = Mesh(mesh.devices.reshape(tensor, dp // tensor, tensor // 2, 2), ("a", "b", "x", "c"))
    matrix = P(("a", "b"), ("x", "c"))
    vector = P(("a", "b", "x", "c"))
    return jax.shard_map(
        on_device,
        mesh=split,
        in_specs=(matrix, P(("a", "b"), None)) + (matrix,) * 7 + (vector, vector, P(), P(), matrix),
        out_specs=(matrix,) * 9 + (vector, vector, P(), P()),
        check_vma=False,
    )
```

```python
import jax
import jax.numpy as jnp
from jax import lax
from jax.sharding import Mesh
from jax.sharding import PartitionSpec as P

epsilon = 1e-06
rope_base = 1000000.0
masked_score = -1e30
f32 = jnp.float32
bf16 = jnp.bfloat16


def shift(value, axis, step):
    size = lax.axis_size(axis)
    return lax.ppermute(value, axis, [(i, (i + step) % size) for i in range(size)])


def flip(value, axis, mask=1):
    return lax.ppermute(value, axis, [(i, i ^ mask) for i in range(lax.axis_size(axis))])


def transpose_blocks(value):
    size = lax.axis_size("a")
    inner = lax.axis_size("c")
    outer = lax.axis_size("x")
    pairs = []
    for a in range(size):
        for t in range(outer * inner):
            pairs.append((a * size + t, t * size + a))
    return lax.ppermute(value, ("a", "x", "c"), pairs)


def ring_sum(value):
    if lax.axis_size("a") != 4:
        return lax.psum(value, "a")
    value = value + flip(value, "a", 1)
    return value + flip(value, "a", 3)


def line(value, pairs):
    return lax.ppermute(value, "a", pairs)


def ring_scatter(partial, held=(), held_two=()):
    return ring_add(jnp.split(partial, 4, axis=0), held, held_two)


def ring_add(blocks, held=(), held_two=()):
    blocks, held = ring_add_first(blocks, held)
    total = ring_add_rest(blocks, held_two)
    if held_two:
        return (total[0], *held, *total[1:])
    return (total, *held) if held else total


def ring_add_first(blocks, held=()):
    zero, one, two, three = blocks
    i = lax.axis_index("a")
    two = two + line(jnp.where(i == 0, three, one), [(0, 1), (3, 2)])
    two, *held = lax.optimization_barrier((two, *held))
    return (zero, one, two, three), held


def ring_add_rest(blocks, held_two=()):
    zero, one, two, three = blocks
    one = one + line(two, [(0, 1), (1, 2)])
    three = three + line(two, [(3, 2), (2, 1)])
    one, three, *held_two = lax.optimization_barrier((one, three, *held_two))
    total = zero + line(one, [(0, 1), (1, 2), (2, 3)]) + line(three, [(3, 2), (2, 1), (1, 0)])
    return (total, *held_two) if held_two else total


def ring_first(own):
    return line(own, [(0, 1), (1, 2), (2, 3)]), line(own, [(3, 2), (2, 1), (1, 0)])


def ring_second(before, behind):
    return line(before, [(1, 2), (2, 3)]), line(behind, [(2, 1), (1, 0)])


def ring_third(before_two, behind_two):
    i = lax.axis_index("a")
    return line(jnp.where(i == 2, before_two, behind_two), [(2, 3), (1, 0)])


def ring_order(own, before, behind, before_two, behind_two, far):
    i = lax.axis_index("a")
    return [
        own,
        jnp.where(i == 3, far, behind),
        jnp.where(i < 2, behind_two, before_two),
        jnp.where(i == 0, far, before),
    ]


def ring_blocks(own):
    first = ring_first(own)
    second = ring_second(*first)
    return ring_order(own, *first, *second, ring_third(*second))


def ring_gather(own, axis=0):
    return jnp.concatenate(ring_blocks(own), axis=axis)


def column_block(value, r):
    size = lax.axis_size("a")
    width = value.shape[1] // size
    return lax.dynamic_slice_in_dim(value, ((lax.axis_index("a") + r) % size) * width, width, 1)


def ring_columns(*values):
    return jnp.concatenate([column_block(value, r) for r in range(4) for value in values], axis=1)


def plain_columns(value, which=0, count=1):
    size = lax.axis_size("a")
    width = value.shape[1] // (size * count)
    a = lax.axis_index("a")
    blocks = []
    for j in range(size):
        at = ((j - a) % size) * count + which
        blocks.append(lax.dynamic_slice_in_dim(value, at * width, width, 1))
    return jnp.concatenate(blocks, axis=1).astype(f32)


def block_for(shards, r):
    blocks = [column_block(shard, (4 - r) % 4) for shard in shards]
    return jnp.concatenate(blocks, axis=1) if len(blocks) > 1 else blocks[0]


def together(*values):
    return lax.optimization_barrier(values)


def line_pieces(own):
    first = ring_first(own)
    second = ring_second(*first)
    far = ring_third(*second)
    two = jnp.where(lax.axis_index("a") < 2, second[1], second[0])
    return [own, first[1], two, first[0], far]


def spread_over_x(*blocks):
    group = jnp.stack(blocks)
    return jnp.stack([group, flip(group, "x")], axis=1)


def spread_over_c(group):
    group = jnp.stack([group, flip(group, "c")], axis=1)
    return [piece.reshape(-1, group.shape[-1]) for piece in group]


def spread_one(block):
    pair = jnp.concatenate([block, flip(block, "x")], axis=0)
    return jnp.concatenate([pair, flip(pair, "c")], axis=0)


def ring_pieces(pieces):
    i = lax.axis_index("a")
    own, one, two, three, far = pieces
    return [own, jnp.where(i == 3, far, one), two, jnp.where(i == 0, far, three)]


def flip_half(partial):
    blocks = partial.reshape(2, 2, partial.shape[0] // 4, partial.shape[1])
    return blocks[0] + flip(blocks[1], "c")


def flip_rest(pair):
    return pair[0] + flip(pair[1], "x")


def tensor_scatter(partial):
    size = lax.axis_size("a")
    a = lax.axis_index("a")
    x = lax.axis_index("x")
    c = lax.axis_index("c")
    rows = partial.shape[0] // size

    def block(t):
        return lax.dynamic_slice_in_dim(partial, ((t - a) % size) * rows, rows)

    send = jnp.stack([block(2 * (1 - x) + 1 - c), block(2 * x + 1 - c)])
    got = flip(send, "c")
    far = block(2 * (1 - x) + c) + got[0]
    near = block(2 * x + c) + got[1]
    return near + flip(far, "x")


def tensor_gather(own, held=()):
    size = lax.axis_size("a")
    a = lax.axis_index("a")
    t = lax.axis_index("x") * 2 + lax.axis_index("c")
    pair, *held = together(jnp.stack([own, flip(own, "x")]), *held)
    other = flip(pair, "c")
    pieces = jnp.stack([pair[0], other[0], pair[1], other[1]])
    gathered = jnp.concatenate(
        [lax.dynamic_index_in_dim(pieces, ((a + r) % size) ^ t, 0, False) for r in range(size)], axis=0
    )
    return (gathered, *held) if held else gathered


def chunk_gains(value):
    if lax.axis_size("b") != 2:
        return lax.all_gather(value, ("b", "x", "c"), axis=0, tiled=False)
    lane = (lax.axis_index("b") * 2 + lax.axis_index("x")) * 2 + lax.axis_index("c")
    total = lax.dynamic_update_slice_in_dim(jnp.zeros((8,) + value.shape, f32), value[None], lane, 0)
    for axis in ("c", "x", "b"):
        total = total + flip(total, axis)
    return total


def fetch(shard):
    return lax.all_gather(shard, "b", axis=0, tiled=True)


def dot(left, right, left_dim, right_dim):
    return lax.dot_general(
        left, right, (((left_dim,), (right_dim,)), ((), ())), preferred_element_type=f32
    )


def project_in(rows, weight):
    return dot(rows, weight, 1, 0)


def project_out(rows, weight):
    return dot(rows, weight, 1, 1)


def project_all(pieces, weights):
    total = project_in(pieces[0], weights[0])
    for r in (1, 3, 2):
        total = total + project_in(pieces[r], weights[r])
    weight = jnp.where(lax.axis_index("a") == 3, weights[1], weights[3])
    total, weight, far = together(total, weight, pieces[4])
    return total + project_in(far, weight)


def weight_partial(rows, grads):
    return dot(rows, grads, 0, 0).astype(bf16)


def pair_scatter(partial):
    return lax.psum_scatter(partial, "b", scatter_dimension=0, tiled=True)


def weight_grad(rows, grads):
    return pair_scatter(weight_partial(rows, grads)).astype(f32)


def rope_tables(segments, head_size):
    rows = segments.shape[1]
    starts = jnp.sum((segments[:, None, :] < segments[:, :, None]).astype(jnp.int32), axis=2)
    position = (jnp.arange(rows, dtype=jnp.int32)[None] - starts).astype(f32)
    half_size = head_size // 2
    frequency = jnp.power(rope_base, -2.0 * jnp.arange(half_size, dtype=f32) / head_size)
    angles = position[:, :, None] * frequency[None, None, :]
    angles = jnp.concatenate([angles, angles], axis=2)
    return (jnp.cos(angles)[:, :, None, :], jnp.sin(angles)[:, :, None, :])


def visible(segments):
    order = jnp.arange(segments.shape[1], dtype=jnp.int32)
    same = segments[:, :, None] == segments[:, None, :]
    return same & (order[:, None] >= order[None, :])[None]


def apply_rotary(value, cosine, sine):
    half = value.shape[-1] // 2
    turned = jnp.concatenate([-value[..., half:], value[..., :half]], axis=-1)
    return value * cosine + turned * sine


def rotate_back(upstream, cosine, sine):
    scaled = upstream * sine
    half = upstream.shape[-1] // 2
    turned = jnp.concatenate([scaled[..., half:], -scaled[..., :half]], axis=-1)
    return upstream * cosine + turned


def norm_back(upstream, normed, inverse, gain):
    scaled = upstream * gain
    return inverse * (scaled - normed * jnp.mean(scaled * normed, axis=-1, keepdims=True))


def attention_forward(qkv, segments, query_gain, key_gain, kv_heads):
    batch, length = segments.shape
    head = query_gain.shape[0]
    kv_width = kv_heads * head
    heads = (qkv.shape[1] - 2 * kv_width) // head
    query_pre = qkv[:, : heads * head].reshape(batch, length, heads, head)
    key_pre = qkv[:, heads * head : heads * head + kv_width].reshape(batch, length, kv_heads, head)
    value = qkv[:, heads * head + kv_width :].astype(bf16).reshape(batch, length, kv_heads, head)
    cosine, sine = rope_tables(segments, head)
    query_inv = lax.rsqrt(jnp.mean(query_pre * query_pre, axis=3, keepdims=True) + epsilon)
    key_inv = lax.rsqrt(jnp.mean(key_pre * key_pre, axis=3, keepdims=True) + epsilon)
    query_rot = apply_rotary(query_pre * query_inv * query_gain, cosine, sine).astype(bf16)
    query_rot = query_rot.reshape(batch, length, kv_heads, heads // kv_heads, head)
    key_rot = apply_rotary(key_pre * key_inv * key_gain, cosine, sine).astype(bf16)
    allowed = visible(segments)[:, None, None]
    scores = jnp.einsum("bqkgd,bskd->bkgqs", query_rot, key_rot, preferred_element_type=f32)
    scores = jnp.where(allowed, scores * head ** (-0.5), masked_score)
    top = jnp.max(scores, axis=4, keepdims=True)
    exps = jnp.exp(scores - top)
    totals = jnp.sum(exps, axis=4, keepdims=True)
    probs = exps / totals
    probs_low = probs.astype(bf16)
    mixed = jnp.einsum("bkgqs,bskd->bqkgd", probs_low, value, preferred_element_type=f32)
    mixed = mixed.astype(bf16).reshape(batch * length, heads * head)
    return mixed, (query_pre, key_pre, value, query_inv, key_inv, query_rot, key_rot, cosine, sine, probs)


def attention_backward(d_mixed, saved, query_gain, key_gain):
    query_pre, key_pre, value, query_inv, key_inv, query_rot, key_rot, cosine, sine, probs = saved
    batch, length, heads, head = query_pre.shape
    scale = head ** (-0.5)
    d_mixed = d_mixed.astype(bf16).reshape(query_rot.shape)
    d_probs = jnp.einsum("bqkgd,bskd->bkgqs", d_mixed, value, preferred_element_type=f32)
    delta = jnp.sum(probs * d_probs, axis=4, keepdims=True)
    d_scores = (probs * (d_probs - delta)).astype(bf16)
    d_value = jnp.einsum("bkgqs,bqkgd->bskd", probs.astype(bf16), d_mixed, preferred_element_type=f32)
    d_query = jnp.einsum("bkgqs,bskd->bqkgd", d_scores, key_rot, preferred_element_type=f32) * scale
    d_query = d_query.reshape(query_pre.shape)
    d_key = jnp.einsum("bkgqs,bqkgd->bskd", d_scores, query_rot, preferred_element_type=f32) * scale
    query_normed = query_pre * query_inv
    key_normed = key_pre * key_inv
    d_query = rotate_back(d_query, cosine, sine)
    d_key = rotate_back(d_key, cosine, sine)
    query_gain_part = jnp.sum(d_query * query_normed, axis=(0, 1, 2))
    key_gain_part = jnp.sum(d_key * key_normed, axis=(0, 1, 2))
    d_query = norm_back(d_query, query_normed, query_inv, query_gain).astype(bf16)
    d_key = norm_back(d_key, key_normed, key_inv, key_gain).astype(bf16)
    rows = batch * length
    d_qkv = jnp.concatenate(
        [d_query.reshape(rows, -1), d_key.reshape(rows, -1), d_value.astype(bf16).reshape(rows, -1)],
        axis=1,
    )
    return d_qkv, query_gain_part, key_gain_part


def on_device(
    tokens,
    segments,
    w_query,
    key_weight,
    value_weight,
    w_out,
    w_gate,
    w_up,
    w_down,
    attn_gain,
    ffn_gain,
    query_gain,
    key_gain,
    cotangent,
):
    size = lax.axis_size("a")
    width = tokens.shape[1] * size
    head = query_gain.shape[0]
    kv_heads = key_weight.shape[1] // head
    query_width = w_query.shape[1]
    kv_width = key_weight.shape[1]

    x_block = transpose_blocks(tokens).astype(f32)
    wqkv = jnp.concatenate([w_query, key_weight, value_weight], axis=1)
    gains, wqkv = together(jnp.stack([attn_gain, ffn_gain]), wqkv)
    wqkv = fetch(wqkv)
    gains = chunk_gains(gains)
    attn_gain = gains[:, 0].reshape(-1)
    ffn_gain = gains[:, 1].reshape(-1)
    inv_one = lax.rsqrt(ring_sum(jnp.sum(x_block * x_block, axis=1, keepdims=True)) / width + epsilon)
    normed_one = x_block * inv_one
    gate_up_blocks = [block_for([w_gate, w_up], r) for r in range(4)]
    down_blocks = [block_for([w_down], r) for r in range(4)]
    hidden_block, *gate_up_blocks = together((normed_one * attn_gain).astype(bf16), *gate_up_blocks)
    near = [shift(gate_up_blocks[r], "a", 4 - r) for r in (1, 3)]
    hidden_one, dy_block = together(tensor_gather(hidden_block), cotangent)
    blocks = jnp.split(project_in(hidden_one, wqkv), 4, axis=0)
    blocks, held = ring_add_first(blocks, (transpose_blocks(dy_block), *near))
    dy_block, near = held[0], held[1:]
    qkv, *dy_line = ring_add_rest(blocks, line_pieces(dy_block))
    wo = fetch(w_out)
    zero, one, three = [fetch(piece) for piece in (gate_up_blocks[0], *near)]
    values = together(qkv, *dy_line, *down_blocks)
    qkv, dy_line, down_blocks = values[0], values[1:6], values[6:]
    down = [shift(down_blocks[r], "a", 4 - r) for r in (1, 2, 3)]
    mixed, saved = attention_forward(qkv, segments, query_gain, key_gain, kv_heads)
    values = together(
        mixed,
        spread_over_x(dy_line[0], dy_line[1], dy_line[3]),
        spread_over_x(dy_line[2], dy_line[4]),
        zero,
        one,
        three,
        gate_up_blocks[2],
        *down,
    )
    mixed = values[0]
    dy_own, dy_one, dy_three = spread_over_c(values[1])
    dy_two, dy_far = spread_over_c(values[2])
    zero, one, three, opposite = values[3:7]
    down = [fetch(piece) for piece in (down_blocks[0], *values[7:])]
    values = together(ring_gather(mixed), opposite, dy_own, dy_one, dy_two, dy_three, dy_far)
    mixed_rows, opposite, dy_pieces = values[0], values[1], values[2:]
    dy_rows = dy_pieces[0]
    opposite = shift(opposite, "a", 2)
    resid, opposite = together(x_block + tensor_scatter(project_out(mixed_rows, wo)), opposite)
    two = fetch(opposite)
    inv_two = lax.rsqrt(ring_sum(jnp.sum(resid * resid, axis=1, keepdims=True)) / width + epsilon)
    normed_two = resid * inv_two
    hidden_block, *down = together((normed_two * ffn_gain).astype(bf16), *down)
    columns = [zero, one, two, three]
    hidden_pieces = [spread_one(piece) for piece in line_pieces(hidden_block)]
    d_act = project_all(dy_pieces, down)
    gate, up = jnp.split(project_all(hidden_pieces, columns), 2, axis=1)
    hidden_pieces = ring_pieces(hidden_pieces)
    wd = fetch(ring_columns(w_down))
    sig = jax.nn.sigmoid(gate)
    act = (gate * sig * up).astype(bf16)
    d_gate = (d_act * up * sig * (1.0 + gate * (1.0 - sig))).astype(bf16)
    d_up = (d_act * (gate * sig)).astype(bf16)
    d_gate_up = jnp.concatenate([d_gate, d_up], axis=1)
    parts = {r: project_out(d_gate_up, columns[r]) for r in (3, 1)}
    parts[3], parts[1], d_gate_up = together(parts[3], parts[1], d_gate_up)
    next_grad = weight_partial(hidden_pieces[1], d_gate_up)
    d_gate_up, next_grad = together(d_gate_up, next_grad)
    next_grad = shift(pair_scatter(next_grad), "a", 1)
    parts.update({r: project_out(d_gate_up, columns[r]) for r in (2, 0)})
    parts = {r: flip_rest(flip_half(parts[r])) for r in (3, 1, 2, 0)}
    parts[3], parts[1], next_grad, *act_first = together(
        parts[3], parts[1], next_grad, *ring_first(act)
    )
    d_hidden_two, *grads = together(
        ring_add([parts[r] for r in range(4)]),
        *[weight_partial(hidden_pieces[r], d_gate_up) for r in (3, 2, 0)],
    )
    last_grad, far_grad, own_grad = [pair_scatter(grad) for grad in grads]
    ffn_gain_part = jnp.sum(d_hidden_two * normed_two, axis=0)
    e_two = d_hidden_two * ffn_gain
    stat_two = ring_sum(jnp.sum(e_two * normed_two, axis=1, keepdims=True)) / width
    d_resid = dy_block.astype(f32) + inv_two * (e_two - normed_two * stat_two)
    d_resid, *act_first = together(d_resid, *act_first)
    act_second = ring_second(*act_first)
    d_resid_rows, *act_second = tensor_gather(d_resid.astype(bf16), act_second)
    d_mixed, wd = together(project_in(d_resid_rows, wo), wd)
    far_parts = jnp.split(far_grad, 4, axis=1)
    d_mixed, grad_out, last_grad, far_parts[0], own_grad, *act_second = together(
        ring_scatter(d_mixed),
        weight_partial(d_resid_rows, mixed_rows),
        last_grad,
        shift(far_parts[0], "a", 2),
        own_grad,
        *act_second,
    )
    grad_out = pair_scatter(grad_out)
    act_third = ring_third(*act_second)
    d_qkv, query_part, key_part = attention_backward(d_mixed, saved, query_gain, key_gain)
    d_qkv, act_third, grad_out = together(d_qkv, act_third, grad_out)
    act_rows = jnp.concatenate(ring_order(act, *act_first, *act_second, act_third), axis=1)
    d_qkv_rows, head_parts, grad_down, ffn_out, last_grad, far_parts[1] = together(
        ring_gather(d_qkv),
        ring_sum(jnp.stack([query_part, key_part])),
        weight_partial(dy_rows, act_rows),
        flip_half(project_out(act_rows, wd)),
        last_grad,
        shift(far_parts[1], "a", 2),
    )
    grad_down = pair_scatter(grad_down)
    grad_out = grad_out.astype(f32)
    d_hidden_one, d_qkv_rows = together(project_out(d_qkv_rows, wqkv), d_qkv_rows)
    d_hidden_one, ffn_out, last_grad, far_parts[2] = together(
        tensor_scatter(d_hidden_one),
        ffn_out,
        shift(last_grad, "a", 3),
        shift(far_parts[2], "a", 2),
    )
    block_out = transpose_blocks((resid + flip_rest(ffn_out)).astype(bf16))
    attn_gain_part = jnp.sum(d_hidden_one * normed_one, axis=0)
    e_one = d_hidden_one * attn_gain
    stat_one = ring_sum(jnp.sum(e_one * normed_one, axis=1, keepdims=True)) / width
    d_tokens = d_resid + inv_one * (e_one - normed_one * stat_one)
    d_tokens, far_parts[3] = together(d_tokens, far_parts[3])
    d_tokens = transpose_blocks(d_tokens)
    grad_qkv = weight_grad(hidden_one, d_qkv_rows)

    gains = jnp.concatenate(
        [attn_gain_part, ffn_gain_part, head_parts.reshape(-1)]
    ).reshape(-1, head)
    gains = gains + flip(gains, "c")
    gains = gains + flip(gains, "x")
    far_parts[3] = shift(far_parts[3], "a", 2)
    grad_gate_up = jnp.concatenate([own_grad, last_grad, *far_parts, next_grad], axis=1)
    grad_gate = plain_columns(grad_gate_up, 0, 2)
    grad_up = plain_columns(grad_gate_up, 1, 2)
    grad_down = plain_columns(grad_down)
    gains = gains + flip(gains, "b") if lax.axis_size("b") == 2 else lax.psum(gains, "b")
    chunk = attn_gain_part.shape[0]
    lane = (lax.axis_index("b") * lax.axis_size("x") + lax.axis_index("x")) * lax.axis_size(
        "c"
    ) + lax.axis_index("c")
    part = chunk // (lax.axis_size("b") * size)
    flat = gains.reshape(-1)
    return (
        block_out,
        d_tokens,
        grad_qkv[:, :query_width],
        grad_qkv[:, query_width : query_width + kv_width],
        grad_qkv[:, query_width + kv_width :],
        grad_out,
        grad_gate,
        grad_up,
        grad_down,
        lax.dynamic_slice_in_dim(flat, lane * part, part),
        lax.dynamic_slice_in_dim(flat, chunk + lane * part, part),
        flat[2 * chunk : 2 * chunk + head],
        flat[2 * chunk + head :],
    )


def solution(mesh):
    dp = mesh.shape["dp"]
    tensor = mesh.shape["tensor"]
    split = Mesh(mesh.devices.reshape(tensor, dp // tensor, tensor // 2, 2), ("a", "b", "x", "c"))
    matrix = P(("a", "b"), ("x", "c"))
    vector = P(("a", "b", "x", "c"))
    return jax.shard_map(
        on_device,
        mesh=split,
        in_specs=(matrix, P(("a", "b"), None)) + (matrix,) * 7 + (vector, vector, P(), P(), matrix),
        out_specs=(matrix,) * 9 + (vector, vector, P(), P()),
        check_vma=False,
    )
```

```python
import jax
import jax.numpy as jnp
from jax import lax
from jax.sharding import Mesh
from jax.sharding import PartitionSpec as P

epsilon = 1e-06
rope_base = 1000000.0
masked_score = -1e30
f32 = jnp.float32
bf16 = jnp.bfloat16


def shift(value, axis, step):
    size = lax.axis_size(axis)
    return lax.ppermute(value, axis, [(i, (i + step) % size) for i in range(size)])


def flip(value, axis, mask=1):
    return lax.ppermute(value, axis, [(i, i ^ mask) for i in range(lax.axis_size(axis))])


def transpose_blocks(value):
    size = lax.axis_size("a")
    inner = lax.axis_size("c")
    outer = lax.axis_size("x")
    pairs = []
    for a in range(size):
        for t in range(outer * inner):
            pairs.append((a * size + t, t * size + a))
    return lax.ppermute(value, ("a", "x", "c"), pairs)


def ring_sum(value):
    if lax.axis_size("a") != 4:
        return lax.psum(value, "a")
    value = value + flip(value, "a", 1)
    return value + flip(value, "a", 3)


def line(value, pairs):
    return lax.ppermute(value, "a", pairs)


def ring_scatter(partial, held=(), held_two=()):
    return ring_add(jnp.split(partial, 4, axis=0), held, held_two)


def ring_add(blocks, held=(), held_two=()):
    blocks, held = ring_add_first(blocks, held)
    total = ring_add_rest(blocks, held_two)
    if held_two:
        return (total[0], *held, *total[1:])
    return (total, *held) if held else total


def ring_add_first(blocks, held=()):
    zero, one, two, three = blocks
    i = lax.axis_index("a")
    two = two + line(jnp.where(i == 0, three, one), [(0, 1), (3, 2)])
    two, *held = lax.optimization_barrier((two, *held))
    return (zero, one, two, three), held


def ring_add_rest(blocks, held_two=()):
    zero, one, two, three = blocks
    one = one + line(two, [(0, 1), (1, 2)])
    three = three + line(two, [(3, 2), (2, 1)])
    one, three, *held_two = lax.optimization_barrier((one, three, *held_two))
    total = zero + line(one, [(0, 1), (1, 2), (2, 3)]) + line(three, [(3, 2), (2, 1), (1, 0)])
    return (total, *held_two) if held_two else total


def ring_first(own):
    return line(own, [(0, 1), (1, 2), (2, 3)]), line(own, [(3, 2), (2, 1), (1, 0)])


def ring_second(before, behind):
    return line(before, [(1, 2), (2, 3)]), line(behind, [(2, 1), (1, 0)])


def ring_third(before_two, behind_two):
    i = lax.axis_index("a")
    return line(jnp.where(i == 2, before_two, behind_two), [(2, 3), (1, 0)])


def ring_order(own, before, behind, before_two, behind_two, far):
    i = lax.axis_index("a")
    return [
        own,
        jnp.where(i == 3, far, behind),
        jnp.where(i < 2, behind_two, before_two),
        jnp.where(i == 0, far, before),
    ]


def ring_blocks(own):
    first = ring_first(own)
    second = ring_second(*first)
    return ring_order(own, *first, *second, ring_third(*second))


def ring_gather(own, axis=0):
    return jnp.concatenate(ring_blocks(own), axis=axis)


def column_block(value, r):
    size = lax.axis_size("a")
    width = value.shape[1] // size
    return lax.dynamic_slice_in_dim(value, ((lax.axis_index("a") + r) % size) * width, width, 1)


def ring_columns(*values):
    return jnp.concatenate([column_block(value, r) for r in range(4) for value in values], axis=1)


def plain_columns(value, which=0, count=1):
    size = lax.axis_size("a")
    width = value.shape[1] // (size * count)
    a = lax.axis_index("a")
    blocks = []
    for j in range(size):
        at = ((j - a) % size) * count + which
        blocks.append(lax.dynamic_slice_in_dim(value, at * width, width, 1))
    return jnp.concatenate(blocks, axis=1).astype(f32)


def block_for(shards, r):
    blocks = [column_block(shard, (4 - r) % 4) for shard in shards]
    return jnp.concatenate(blocks, axis=1) if len(blocks) > 1 else blocks[0]


def together(*values):
    return lax.optimization_barrier(values)


def line_pieces(own):
    first = ring_first(own)
    second = ring_second(*first)
    far = ring_third(*second)
    two = jnp.where(lax.axis_index("a") < 2, second[1], second[0])
    return [own, first[1], two, first[0], far]


def spread_over_x(*blocks):
    group = jnp.stack(blocks)
    return jnp.stack([group, flip(group, "x")], axis=1)


def spread_over_c(group):
    group = jnp.stack([group, flip(group, "c")], axis=1)
    return [piece.reshape(-1, group.shape[-1]) for piece in group]


def spread_one(block):
    pair = jnp.concatenate([block, flip(block, "x")], axis=0)
    return jnp.concatenate([pair, flip(pair, "c")], axis=0)


def ring_pieces(pieces):
    i = lax.axis_index("a")
    own, one, two, three, far = pieces
    return [own, jnp.where(i == 3, far, one), two, jnp.where(i == 0, far, three)]


def flip_half(partial):
    blocks = partial.reshape(2, 2, partial.shape[0] // 4, partial.shape[1])
    return blocks[0] + flip(blocks[1], "c")


def flip_rest(pair):
    return pair[0] + flip(pair[1], "x")


def tensor_scatter(partial):
    size = lax.axis_size("a")
    a = lax.axis_index("a")
    x = lax.axis_index("x")
    c = lax.axis_index("c")
    rows = partial.shape[0] // size

    def block(t):
        return lax.dynamic_slice_in_dim(partial, ((t - a) % size) * rows, rows)

    send = jnp.stack([block(2 * (1 - x) + 1 - c), block(2 * x + 1 - c)])
    got = flip(send, "c")
    far = block(2 * (1 - x) + c) + got[0]
    near = block(2 * x + c) + got[1]
    return near + flip(far, "x")


def tensor_gather(own, held=()):
    size = lax.axis_size("a")
    a = lax.axis_index("a")
    t = lax.axis_index("x") * 2 + lax.axis_index("c")
    pair, *held = together(jnp.stack([own, flip(own, "x")]), *held)
    other = flip(pair, "c")
    pieces = jnp.stack([pair[0], other[0], pair[1], other[1]])
    gathered = jnp.concatenate(
        [lax.dynamic_index_in_dim(pieces, ((a + r) % size) ^ t, 0, False) for r in range(size)], axis=0
    )
    return (gathered, *held) if held else gathered


def chunk_gains(value):
    if lax.axis_size("b") != 2:
        return lax.all_gather(value, ("b", "x", "c"), axis=0, tiled=False)
    lane = (lax.axis_index("b") * 2 + lax.axis_index("x")) * 2 + lax.axis_index("c")
    total = lax.dynamic_update_slice_in_dim(jnp.zeros((8,) + value.shape, f32), value[None], lane, 0)
    for axis in ("c", "x", "b"):
        total = total + flip(total, axis)
    return total


def fetch(shard):
    return lax.all_gather(shard, "b", axis=0, tiled=True)


def dot(left, right, left_dim, right_dim):
    return lax.dot_general(
        left, right, (((left_dim,), (right_dim,)), ((), ())), preferred_element_type=f32
    )


def project_in(rows, weight):
    return dot(rows, weight, 1, 0)


def project_out(rows, weight):
    return dot(rows, weight, 1, 1)


def project_all(pieces, weights):
    total = project_in(pieces[0], weights[0])
    for r in (1, 3, 2):
        total = total + project_in(pieces[r], weights[r])
    weight = jnp.where(lax.axis_index("a") == 3, weights[1], weights[3])
    total, weight, far = together(total, weight, pieces[4])
    return total + project_in(far, weight)


def weight_partial(rows, grads):
    return dot(rows, grads, 0, 0).astype(bf16)


def pair_scatter(partial):
    return lax.psum_scatter(partial, "b", scatter_dimension=0, tiled=True)


def weight_grad(rows, grads):
    return pair_scatter(weight_partial(rows, grads)).astype(f32)


def rope_tables(segments, head_size):
    rows = segments.shape[1]
    starts = jnp.sum((segments[:, None, :] < segments[:, :, None]).astype(jnp.int32), axis=2)
    position = (jnp.arange(rows, dtype=jnp.int32)[None] - starts).astype(f32)
    half_size = head_size // 2
    frequency = jnp.power(rope_base, -2.0 * jnp.arange(half_size, dtype=f32) / head_size)
    angles = position[:, :, None] * frequency[None, None, :]
    angles = jnp.concatenate([angles, angles], axis=2)
    return (jnp.cos(angles)[:, :, None, :], jnp.sin(angles)[:, :, None, :])


def visible(segments):
    order = jnp.arange(segments.shape[1], dtype=jnp.int32)
    same = segments[:, :, None] == segments[:, None, :]
    return same & (order[:, None] >= order[None, :])[None]


def apply_rotary(value, cosine, sine):
    half = value.shape[-1] // 2
    turned = jnp.concatenate([-value[..., half:], value[..., :half]], axis=-1)
    return value * cosine + turned * sine


def rotate_back(upstream, cosine, sine):
    scaled = upstream * sine
    half = upstream.shape[-1] // 2
    turned = jnp.concatenate([scaled[..., half:], -scaled[..., :half]], axis=-1)
    return upstream * cosine + turned


def norm_back(upstream, normed, inverse, gain):
    scaled = upstream * gain
    return inverse * (scaled - normed * jnp.mean(scaled * normed, axis=-1, keepdims=True))


def attention_forward(qkv, segments, query_gain, key_gain, kv_heads):
    batch, length = segments.shape
    head = query_gain.shape[0]
    kv_width = kv_heads * head
    heads = (qkv.shape[1] - 2 * kv_width) // head
    query_pre = qkv[:, : heads * head].reshape(batch, length, heads, head)
    key_pre = qkv[:, heads * head : heads * head + kv_width].reshape(batch, length, kv_heads, head)
    value = qkv[:, heads * head + kv_width :].astype(bf16).reshape(batch, length, kv_heads, head)
    cosine, sine = rope_tables(segments, head)
    query_inv = lax.rsqrt(jnp.mean(query_pre * query_pre, axis=3, keepdims=True) + epsilon)
    key_inv = lax.rsqrt(jnp.mean(key_pre * key_pre, axis=3, keepdims=True) + epsilon)
    query_rot = apply_rotary(query_pre * query_inv * query_gain, cosine, sine).astype(bf16)
    query_rot = query_rot.reshape(batch, length, kv_heads, heads // kv_heads, head)
    key_rot = apply_rotary(key_pre * key_inv * key_gain, cosine, sine).astype(bf16)
    allowed = visible(segments)[:, None, None]
    scores = jnp.einsum("bqkgd,bskd->bkgqs", query_rot, key_rot, preferred_element_type=f32)
    scores = jnp.where(allowed, scores * head ** (-0.5), masked_score)
    top = jnp.max(scores, axis=4, keepdims=True)
    exps = jnp.exp(scores - top)
    totals = jnp.sum(exps, axis=4, keepdims=True)
    probs = exps / totals
    probs_low = probs.astype(bf16)
    mixed = jnp.einsum("bkgqs,bskd->bqkgd", probs_low, value, preferred_element_type=f32)
    mixed = mixed.astype(bf16).reshape(batch * length, heads * head)
    return mixed, (query_pre, key_pre, value, query_inv, key_inv, query_rot, key_rot, cosine, sine, probs)


def attention_backward(d_mixed, saved, query_gain, key_gain):
    query_pre, key_pre, value, query_inv, key_inv, query_rot, key_rot, cosine, sine, probs = saved
    batch, length, heads, head = query_pre.shape
    scale = head ** (-0.5)
    d_mixed = d_mixed.astype(bf16).reshape(query_rot.shape)
    d_probs = jnp.einsum("bqkgd,bskd->bkgqs", d_mixed, value, preferred_element_type=f32)
    delta = jnp.sum(probs * d_probs, axis=4, keepdims=True)
    d_scores = (probs * (d_probs - delta)).astype(bf16)
    d_value = jnp.einsum("bkgqs,bqkgd->bskd", probs.astype(bf16), d_mixed, preferred_element_type=f32)
    d_query = jnp.einsum("bkgqs,bskd->bqkgd", d_scores, key_rot, preferred_element_type=f32) * scale
    d_query = d_query.reshape(query_pre.shape)
    d_key = jnp.einsum("bkgqs,bqkgd->bskd", d_scores, query_rot, preferred_element_type=f32) * scale
    query_normed = query_pre * query_inv
    key_normed = key_pre * key_inv
    d_query = rotate_back(d_query, cosine, sine)
    d_key = rotate_back(d_key, cosine, sine)
    query_gain_part = jnp.sum(d_query * query_normed, axis=(0, 1, 2))
    key_gain_part = jnp.sum(d_key * key_normed, axis=(0, 1, 2))
    d_query = norm_back(d_query, query_normed, query_inv, query_gain).astype(bf16)
    d_key = norm_back(d_key, key_normed, key_inv, key_gain).astype(bf16)
    rows = batch * length
    d_qkv = jnp.concatenate(
        [d_query.reshape(rows, -1), d_key.reshape(rows, -1), d_value.astype(bf16).reshape(rows, -1)],
        axis=1,
    )
    return d_qkv, query_gain_part, key_gain_part


def on_device(
    tokens,
    segments,
    w_query,
    key_weight,
    value_weight,
    w_out,
    w_gate,
    w_up,
    w_down,
    attn_gain,
    ffn_gain,
    query_gain,
    key_gain,
    cotangent,
):
    size = lax.axis_size("a")
    width = tokens.shape[1] * size
    head = query_gain.shape[0]
    kv_heads = key_weight.shape[1] // head
    query_width = w_query.shape[1]
    kv_width = key_weight.shape[1]

    x_block = transpose_blocks(tokens).astype(f32)
    wqkv = jnp.concatenate([w_query, key_weight, value_weight], axis=1)
    gains, wqkv = together(jnp.stack([attn_gain, ffn_gain]), wqkv)
    wqkv = fetch(wqkv)
    gains = chunk_gains(gains)
    attn_gain = gains[:, 0].reshape(-1)
    ffn_gain = gains[:, 1].reshape(-1)
    inv_one = lax.rsqrt(ring_sum(jnp.sum(x_block * x_block, axis=1, keepdims=True)) / width + epsilon)
    normed_one = x_block * inv_one
    gate_up_blocks = [block_for([w_gate, w_up], r) for r in range(4)]
    down_blocks = [block_for([w_down], r) for r in range(4)]
    hidden_block, *gate_up_blocks = together((normed_one * attn_gain).astype(bf16), *gate_up_blocks)
    near = [shift(gate_up_blocks[r], "a", 4 - r) for r in (1, 3)]
    hidden_one, dy_block = together(tensor_gather(hidden_block), cotangent)
    blocks = jnp.split(project_in(hidden_one, wqkv), 4, axis=0)
    blocks, held = ring_add_first(blocks, (transpose_blocks(dy_block), *near))
    dy_block, near = held[0], held[1:]
    qkv, *dy_line = ring_add_rest(blocks, line_pieces(dy_block))
    wo = fetch(w_out)
    zero, one, three = [fetch(piece) for piece in (gate_up_blocks[0], *near)]
    values = together(qkv, *dy_line, *down_blocks)
    qkv, dy_line, down_blocks = values[0], values[1:6], values[6:]
    down = [shift(down_blocks[r], "a", 4 - r) for r in (1, 2, 3)]
    mixed, saved = attention_forward(qkv, segments, query_gain, key_gain, kv_heads)
    values = together(
        mixed,
        spread_over_x(dy_line[0], dy_line[1], dy_line[3]),
        spread_over_x(dy_line[2], dy_line[4]),
        zero,
        one,
        three,
        gate_up_blocks[2],
        *down,
    )
    mixed = values[0]
    dy_own, dy_one, dy_three = spread_over_c(values[1])
    dy_two, dy_far = spread_over_c(values[2])
    zero, one, three, opposite = values[3:7]
    down = [fetch(piece) for piece in (down_blocks[0], *values[7:])]
    values = together(ring_gather(mixed), opposite, dy_own, dy_one, dy_two, dy_three, dy_far)
    mixed_rows, opposite, dy_pieces = values[0], values[1], values[2:]
    dy_rows = dy_pieces[0]
    opposite = shift(opposite, "a", 2)
    resid, opposite = together(x_block + tensor_scatter(project_out(mixed_rows, wo)), opposite)
    two = fetch(opposite)
    inv_two = lax.rsqrt(ring_sum(jnp.sum(resid * resid, axis=1, keepdims=True)) / width + epsilon)
    normed_two = resid * inv_two
    hidden_block, *down = together((normed_two * ffn_gain).astype(bf16), *down)
    columns = [zero, one, two, three]
    hidden_pieces = [spread_one(piece) for piece in line_pieces(hidden_block)]
    d_act = project_all(dy_pieces, down)
    gate, up = jnp.split(project_all(hidden_pieces, columns), 2, axis=1)
    hidden_pieces = ring_pieces(hidden_pieces)
    wd = fetch(ring_columns(w_down))
    sig = jax.nn.sigmoid(gate)
    act = (gate * sig * up).astype(bf16)
    d_gate = (d_act * up * sig * (1.0 + gate * (1.0 - sig))).astype(bf16)
    d_up = (d_act * (gate * sig)).astype(bf16)
    d_gate_up = jnp.concatenate([d_gate, d_up], axis=1)
    parts = {r: project_out(d_gate_up, columns[r]) for r in (3, 1)}
    parts[3], parts[1], d_gate_up = together(parts[3], parts[1], d_gate_up)
    next_grad = weight_partial(hidden_pieces[1], d_gate_up)
    d_gate_up, next_grad = together(d_gate_up, next_grad)
    next_grad = shift(pair_scatter(next_grad), "a", 1)
    parts.update({r: project_out(d_gate_up, columns[r]) for r in (2, 0)})
    parts = {r: flip_rest(flip_half(parts[r])) for r in (3, 1, 2, 0)}
    parts[3], parts[1], next_grad, *act_first = together(
        parts[3], parts[1], next_grad, *ring_first(act)
    )
    d_hidden_two, *grads = together(
        ring_add([parts[r] for r in range(4)]),
        *[weight_partial(hidden_pieces[r], d_gate_up) for r in (3, 2, 0)],
    )
    last_grad, far_grad, own_grad = [pair_scatter(grad) for grad in grads]
    ffn_gain_part = jnp.sum(d_hidden_two * normed_two, axis=0)
    e_two = d_hidden_two * ffn_gain
    stat_two = ring_sum(jnp.sum(e_two * normed_two, axis=1, keepdims=True)) / width
    d_resid = dy_block.astype(f32) + inv_two * (e_two - normed_two * stat_two)
    d_resid, *act_first = together(d_resid, *act_first)
    act_second = ring_second(*act_first)
    d_resid_rows, *act_second = tensor_gather(d_resid.astype(bf16), act_second)
    d_mixed, wd = together(project_in(d_resid_rows, wo), wd)
    far_parts = jnp.split(far_grad, 4, axis=1)
    d_mixed, grad_out, last_grad, far_parts[0], own_grad, *act_second = together(
        ring_scatter(d_mixed),
        weight_partial(d_resid_rows, mixed_rows),
        last_grad,
        shift(far_parts[0], "a", 2),
        own_grad,
        *act_second,
    )
    grad_out = pair_scatter(grad_out)
    act_third = ring_third(*act_second)
    d_qkv, query_part, key_part = attention_backward(d_mixed, saved, query_gain, key_gain)
    d_qkv, act_third, grad_out, far_parts[3] = together(
        d_qkv, act_third, grad_out, shift(far_parts[3], "a", 2)
    )
    act_rows = jnp.concatenate(ring_order(act, *act_first, *act_second, act_third), axis=1)
    d_qkv_rows, grad_down, ffn_out, last_grad, far_parts[1] = together(
        ring_gather(d_qkv),
        weight_partial(dy_rows, act_rows),
        flip_half(project_out(act_rows, wd)),
        last_grad,
        shift(far_parts[1], "a", 2),
    )
    grad_down = pair_scatter(grad_down)
    grad_out = grad_out.astype(f32)
    d_hidden_one, d_qkv_rows = together(project_out(d_qkv_rows, wqkv), d_qkv_rows)
    d_hidden_one, ffn_out, last_grad, far_parts[2] = together(
        tensor_scatter(d_hidden_one),
        ffn_out,
        shift(last_grad, "a", 3),
        shift(far_parts[2], "a", 2),
    )
    block_out = transpose_blocks((resid + flip_rest(ffn_out)).astype(bf16))
    attn_gain_part = jnp.sum(d_hidden_one * normed_one, axis=0)
    e_one = d_hidden_one * attn_gain
    stat_one = jnp.sum(e_one * normed_one, axis=1)
    rows = stat_one.shape[0]
    sums = ring_sum(jnp.concatenate([stat_one, query_part, key_part]))
    stat_one = sums[:rows, None] / width
    head_parts = sums[rows:]
    d_tokens = d_resid + inv_one * (e_one - normed_one * stat_one)
    d_tokens = transpose_blocks(d_tokens)
    grad_qkv = weight_grad(hidden_one, d_qkv_rows)

    gains = jnp.concatenate(
        [attn_gain_part, ffn_gain_part, head_parts]
    ).reshape(-1, head)
    gains = gains + flip(gains, "c")
    gains = gains + flip(gains, "x")
    grad_gate_up = jnp.concatenate([own_grad, last_grad, *far_parts, next_grad], axis=1)
    grad_gate = plain_columns(grad_gate_up, 0, 2)
    grad_up = plain_columns(grad_gate_up, 1, 2)
    grad_down = plain_columns(grad_down)
    gains = gains + flip(gains, "b") if lax.axis_size("b") == 2 else lax.psum(gains, "b")
    chunk = attn_gain_part.shape[0]
    lane = (lax.axis_index("b") * lax.axis_size("x") + lax.axis_index("x")) * lax.axis_size(
        "c"
    ) + lax.axis_index("c")
    part = chunk // (lax.axis_size("b") * size)
    flat = gains.reshape(-1)
    return (
        block_out,
        d_tokens,
        grad_qkv[:, :query_width],
        grad_qkv[:, query_width : query_width + kv_width],
        grad_qkv[:, query_width + kv_width :],
        grad_out,
        grad_gate,
        grad_up,
        grad_down,
        lax.dynamic_slice_in_dim(flat, lane * part, part),
        lax.dynamic_slice_in_dim(flat, chunk + lane * part, part),
        flat[2 * chunk : 2 * chunk + head],
        flat[2 * chunk + head :],
    )


def solution(mesh):
    dp = mesh.shape["dp"]
    tensor = mesh.shape["tensor"]
    split = Mesh(mesh.devices.reshape(tensor, dp // tensor, tensor // 2, 2), ("a", "b", "x", "c"))
    matrix = P(("a", "b"), ("x", "c"))
    vector = P(("a", "b", "x", "c"))
    return jax.shard_map(
        on_device,
        mesh=split,
        in_specs=(matrix, P(("a", "b"), None)) + (matrix,) * 7 + (vector, vector, P(), P(), matrix),
        out_specs=(matrix,) * 9 + (vector, vector, P(), P()),
        check_vma=False,
    )
```
